256 devices in a mesh: grp: 8 (over x, core), dev: 32 (over z, y).
Axes of the slice: x: 4, y: 4, z: 8, core: 2. Of those that a mesh axis runs over, the one named last changes fastest.
Arguments:
- amplitudes: bfloat16 [256, 128, 128], P(('grp', 'dev')), may hold values from -2 to 2
- bases: bfloat16 [256, 256, 128], P(('grp', 'dev')), may hold values from -0.375 to 0.375
- factors: bfloat16 [256, 32, 256, 256], P(('grp', 'dev')), may hold values from -0.1875 to 0.1875
- intersections: bfloat16 [256, 4, 128, 128], P(('grp', 'dev')), may hold values from -0.25 to 0.25
- pair_integrals: float32 [256, 128, 128], P(('grp', 'dev')), may hold values from -6 to 6
- pno_energies: float32 [256, 128], P(('grp', 'dev')), may hold values from 0.3 to 3
- pair_shift: float32 [256], P(('grp', 'dev')), may hold values from 0.5 to 4
- pair_atoms: int32 [256, 2], P('grp'), may hold values from 0 to 31, all different within a row; in each aligned block of 32 rows (0 to 31, 32 to 63, ...) at most 3 rows name the same one
- pair_next: int32 [256, 4], P(('grp', 'dev')), may hold values from 0 to 63, as said below
Outputs:
- new_amplitudes: float32 [256, 128, 128], P(('grp', 'dev'))
The draws below stay inside these ranges and needn't reach their ends.
Inputs may be any that keep to these rules, and one draw needn't show every extreme that they name: `pair_atoms`: each pair lists 2 different atoms of its own group. Within a group no atom is listed by more than 3 pairs, and some atom is listed by exactly 3 pairs of its group. `pair_next`: each pair lists 4 different pairs other than itself; a number below 32 is a pair of its own group, a number m from 32 on is pair m - 32 of the next group. Pairs of the last group list only pairs of their own group.
All inputs are finite; a program needn't handle non-finite values.
Results may differ from the reference program's by a relative error of at most 0.008.
Values may be sent and summed in bfloat16 or wider, within the bound.
A program may use at most 128 MiB of HBM per device.

```python
import math
import jax
import jax.numpy as jnp
import numpy as np
from jax import lax

NPNO = 128
NPAO = 256
KAUX = 32
DOM = 2
CAP = 3
NOV = 4
ITERS = 2
GROUPS = 8
PAIR_GRP = 32
PAIRS = 256
ATOMS = 256


def draw_pair_next(key, part):
    row_ids = jnp.arange(PAIRS, dtype=jnp.int32)
    local_index = row_ids % PAIR_GRP
    group_index = row_ids // PAIR_GRP
    candidates = jnp.arange(2 * PAIR_GRP, dtype=jnp.int32)
    scores = jax.random.randint(key, (PAIRS, 2 * PAIR_GRP), 0, 2 ** 20, dtype=jnp.int32) * (4 * PAIR_GRP) + candidates[None, :]
    excluded = (candidates[None, :] == local_index[:, None]) | (group_index[:, None] == GROUPS - 1) & (candidates[None, :] >= PAIR_GRP)
    scores = jnp.where(excluded, -1, scores)
    top_scores, picked = lax.top_k(scores, NOV)
    return picked.astype(jnp.int32)


def block_levels(rng, extent, split, least, largest):
    level, own = 1.0, jax.random.fold_in(rng, 6)
    for position, parts in split:
        draws = jnp.exp(jax.random.uniform(jax.random.fold_in(own, position), (parts,), jnp.float32, least / len(split), largest / len(split)))
        level = level * jnp.repeat(draws, extent[position] // parts).reshape([-1 if axis == position else 1 for axis in range(len(extent))])
    return level


def shared_out(key, own, number, rows, count, top, most, skew):
    ranking = jax.random.permutation(key, count)
    heavy_load, usual = shares(count, rows * top, most, skew, True), shares(count, rows * top, most, skew, False)
    places = jnp.arange(count)

    def named(lengths, rotation):
        used = int((lengths > 0).sum())
        fixed = max(1, used // 4)
        moved = fixed + (places - fixed + rotation * (used - fixed)) % max(1, count - fixed)
        return jnp.zeros((count,), jnp.int32).at[ranking[jnp.where(places < fixed, places, moved)]].set(jnp.asarray(lengths, jnp.int32))

    lengths = jnp.where(number % 4 == 0, named(heavy_load, number // 4), named(usual, number - number // 4 - 1))
    mixed = jax.random.permutation(jax.random.fold_in(own, 3), count)
    donor, sink = mixed[0:count // 2 * 2:2], mixed[1:count // 2 * 2:2]
    slack = jnp.minimum(lengths[donor] - 1, most - lengths[sink]) // 2
    slack = jnp.where((donor == ranking[0]) | (sink == ranking[0]) | (lengths[sink] == 0), 0, jnp.maximum(slack, 0))
    moved = jax.random.randint(jax.random.fold_in(own, 4), (count // 2,), 0, 1 << 20) % (slack + 1)
    lengths = lengths.at[donor].add(-moved).at[sink].add(moved)
    items = jnp.searchsorted(jnp.cumsum(lengths), jnp.arange(rows * top), side="right").astype(jnp.int32)
    grid = items.reshape(top, rows).T
    grid = grid[jax.random.permutation(jax.random.fold_in(own, 1), rows)]
    rotation = jax.random.randint(jax.random.fold_in(own, 2), (rows, 1), 0, top)
    return jnp.take_along_axis(grid, (jnp.arange(top)[None, :] + rotation) % top, axis=1)


def shares(count, total, reach, lean, full):
    loads = [(1 << 20) // math.isqrt(rank ** lean) + 1 for rank in range(1, count + 1)]
    largest = reach if full else min(reach, max(-(-total // count), total * loads[0] // sum(loads)))
    least = 1 if total - largest >= count - 1 else 0
    holding, spare = [largest] + [least] * (count - 1), total - largest - least * (count - 1)
    while spare > 0:
        free = [i for i in range(1, count) if holding[i] < largest] or [i for i in range(1, count) if holding[i] < reach]
        pool, budget = sum([loads[i] for i in free]), spare
        for i in free:
            extra = min(reach - holding[i], max(1, budget * loads[i] // pool), spare)
            holding[i] = holding[i] + extra
            spare = spare - extra
    return np.array(holding)


def scatter_about(key, shape, spread, most, cuts=(), kind=jnp.bfloat16):
    drawn = jax.random.normal(key, shape, jnp.float32) * spread
    if len(cuts) > 0:
        drawn = block_levels(key, shape, cuts, -0.22, 0.18) * drawn
    return jnp.clip(drawn, min=-most, max=most).astype(kind)


def setup_inputs(seed: int = 0) -> dict:
    streams_of = jax.random.split(jax.random.key(seed), 10)
    amplitudes = scatter_about(streams_of[0], (PAIRS, NPNO, NPNO), 0.3, 2.0, ((0, 256),))
    bases = scatter_about(streams_of[1], (PAIRS, NPAO, NPNO), NPAO ** -0.5, 0.375, ((0, 256),))
    factors = scatter_about(streams_of[2], (ATOMS, KAUX, NPAO, NPAO), (4 * NPAO) ** -0.5, 0.1875, ((0, 256),))
    intersections = scatter_about(streams_of[3], (PAIRS, NOV, NPNO, NPNO), (4 * NPNO) ** -0.5, 0.25, ((0, 256),))
    pair_integrals = scatter_about(streams_of[4], (PAIRS, NPNO, NPNO), 1.0, 6.0, ((0, 256),), jnp.float32)
    pno_energies = jnp.clip(jnp.exp(math.log(3.0) - 2.3025851 * jax.random.uniform(streams_of[5], (PAIRS, NPNO), jnp.float32) ** block_levels(streams_of[5], (PAIRS, NPNO), ((0, 256),), -0.2, 0.2)), 0.3, 3.0)
    pair_shift = jnp.clip(jnp.exp(math.log(4.0) - 2.0794415 * jax.random.uniform(streams_of[6], (PAIRS,), jnp.float32) ** block_levels(streams_of[6], (PAIRS,), ((0, 256),), -0.2, 0.2)), 0.5, 4.0)
    pair_atoms_keys = jax.random.split(jax.random.fold_in(streams_of[7], 1), PAIRS // PAIR_GRP)
    pair_atoms_turns = jax.random.permutation(jax.random.fold_in(streams_of[7], 3), PAIRS // PAIR_GRP)
    pair_atoms = jax.vmap(lambda own, number: shared_out(jax.random.fold_in(streams_of[7], 2), own, number, PAIR_GRP, PAIR_GRP, DOM, CAP, 1))(pair_atoms_keys, pair_atoms_turns).reshape((PAIRS, DOM))
    pair_next = draw_pair_next(jax.random.fold_in(streams_of[9], 71), 0)
    return {"amplitudes": amplitudes, "bases": bases, "factors": factors, "intersections": intersections, "pair_integrals": pair_integrals, "pno_energies": pno_energies, "pair_shift": pair_shift, "pair_atoms": pair_atoms, "pair_next": pair_next}


def sandwich(factor_block, expanded):
    aux_count = factor_block.shape[0]
    pao_width = factor_block.shape[1]
    flat_factor = factor_block.reshape(aux_count * pao_width, pao_width)
    squeezed = jnp.dot(flat_factor, expanded, preferred_element_type=jnp.float32).astype(jnp.bfloat16)
    squeezed = squeezed.reshape(aux_count, pao_width, pao_width)
    return jnp.einsum('kad,kbd->ab', squeezed.astype(jnp.float32), factor_block.astype(jnp.float32))


def reference(amplitudes, bases, factors, intersections, pair_integrals, pno_energies, pair_shift, pair_atoms, pair_next):
    starts = (jnp.arange(PAIRS, dtype=jnp.int32) // PAIR_GRP) * PAIR_GRP
    atom_ids = (pair_atoms + starts[:, None]).astype(jnp.int32)
    near_ids = (pair_next + starts[:, None]).astype(jnp.int32)
    denominator = pno_energies[:, :, None] + pno_energies[:, None, :] + pair_shift[:, None, None]
    current = amplitudes
    update = None
    for iteration in range(ITERS):
        def one_pair(pair_index):
            pair_base = bases[pair_index]
            halfway = jnp.dot(pair_base, current[pair_index], preferred_element_type=jnp.float32).astype(jnp.bfloat16)
            expanded = jnp.dot(halfway, pair_base.T, preferred_element_type=jnp.float32).astype(jnp.bfloat16)

            def one_atom(running, atom_index):
                return running + sandwich(factors[atom_index], expanded), None

            ladder_pao, unused = lax.scan(one_atom, jnp.zeros((NPAO, NPAO), jnp.float32), atom_ids[pair_index])
            base_wide = pair_base.astype(jnp.float32)
            left_side = jnp.dot(base_wide.T, ladder_pao, precision=lax.Precision.HIGHEST)
            ladder = jnp.dot(left_side, base_wide, precision=lax.Precision.HIGHEST)
            neighbours = current[near_ids[pair_index]].astype(jnp.float32)
            pair_intersections = intersections[pair_index].astype(jnp.float32)
            mixed = jnp.einsum('nij,njk->nik', pair_intersections, neighbours).astype(jnp.bfloat16)
            coupling = jnp.einsum('nik,nlk->il', mixed.astype(jnp.float32), pair_intersections)
            return -(pair_integrals[pair_index] + ladder + coupling) / denominator[pair_index]

        update = lax.map(one_pair, jnp.arange(PAIRS, dtype=jnp.int32))
        if iteration + 1 < ITERS:
            current = update.astype(jnp.bfloat16)
    return update
```

```python
import jax
import jax.numpy as jnp
from jax import lax
from jax.sharding import PartitionSpec as P

CAP = 3
ITERS = 2


def from_behind(value, axis, steps):
    count = lax.axis_size(axis)
    first, last = (max(0, -steps), min(count, count - steps))
    return lax.ppermute(value, axis, [(source, source + steps) for source in range(first, last)])


def select_rows(selector, stacked):
    flat_rows = stacked.reshape(stacked.shape[0], -1)
    picked = jnp.dot(selector, flat_rows, preferred_element_type=jnp.float32).astype(jnp.bfloat16)
    return picked.reshape((selector.shape[0],) + stacked.shape[1:])


def on_device(
    amplitudes,
    bases,
    factors,
    intersections,
    pair_integrals,
    pno_energies,
    pair_shift,
    pair_atoms,
    pair_next,
):
    local_atom = lax.axis_index("dev")
    group_size = lax.axis_size("dev")
    listed = jnp.sum((pair_atoms == local_atom).astype(jnp.int32), axis=1)
    earlier = jnp.cumsum(listed) - listed
    slot_ids = lax.iota(jnp.int32, CAP)
    selector = ((listed[None, :] == 1) & (earlier[None, :] == slot_ids[:, None])).astype(
        jnp.bfloat16
    )
    factor_block = factors[0]
    denominator = pno_energies[0][:, None] + pno_energies[0][None, :] + pair_shift[0]
    positions = lax.iota(jnp.int32, 2 * group_size)
    picker = (pair_next[0][:, None] == positions[None, :]).astype(jnp.bfloat16)
    pair_intersections = intersections[0]
    slot_bases = select_rows(selector, lax.all_gather(bases, "dev", axis=0, tiled=True))
    half = jnp.einsum(
        "sai,kad->ksid", slot_bases, factor_block, preferred_element_type=jnp.float32
    ).astype(jnp.bfloat16)
    inner = jnp.einsum(
        "ksid,sdj->skij", half, slot_bases, preferred_element_type=jnp.float32
    ).astype(jnp.bfloat16)
    current = amplitudes
    update = None
    for iteration in range(ITERS):
        group_amps = lax.all_gather(current, "dev", axis=0, tiled=True)
        slot_amps = select_rows(selector, group_amps)
        left = jnp.einsum(
            "skij,sjl->skil", inner, slot_amps, preferred_element_type=jnp.float32
        ).astype(jnp.bfloat16)
        terms = jnp.einsum(
            "skil,skml->sim", left, inner, preferred_element_type=jnp.float32
        ).astype(jnp.bfloat16)
        spread = select_rows(selector.T, terms)
        arrived = lax.all_to_all(spread, "dev", split_axis=0, concat_axis=0, tiled=True)
        ladder = jnp.sum(arrived.astype(jnp.float32), axis=0)
        next_amps = from_behind(group_amps, "grp", -1)
        candidates = jnp.concatenate([group_amps, next_amps], axis=0)
        neighbours = select_rows(picker, candidates)
        mixed = jnp.einsum(
            "nij,njk->nik", pair_intersections, neighbours, preferred_element_type=jnp.float32
        ).astype(jnp.bfloat16)
        coupling = jnp.einsum(
            "nik,nlk->il", mixed, pair_intersections, preferred_element_type=jnp.float32
        )
        update = -(pair_integrals[0] + ladder + coupling) / denominator
        if iteration + 1 < ITERS:
            current = update.astype(jnp.bfloat16)[None]
    return update[None]


def solution(mesh):
    return jax.shard_map(
        on_device,
        mesh=mesh,
        in_specs=(
            P(("grp", "dev"), None, None),
            P(("grp", "dev"), None, None),
            P(("grp", "dev"), None, None, None),
            P(("grp", "dev"), None, None, None),
            P(("grp", "dev"), None, None),
            P(("grp", "dev"), None),
            P(("grp", "dev")),
            P("grp", None),
            P(("grp", "dev"), None),
        ),
        out_specs=P(("grp", "dev"), None, None),
        check_vma=False,
    )
```

```python
import jax
import jax.numpy as jnp
from jax import lax
from jax.experimental import pallas as pl
from jax.experimental.pallas import tpu as pltpu
from jax.sharding import PartitionSpec as P

CAP = 3
ITERS = 2
NZ = 8
NY = 4
NOV = 4
F32 = jnp.float32
BF16 = jnp.bfloat16
MESH = pl.DeviceIdType.MESH
Z_ORDER = (4, 3, 5, 2, 6, 1, 7)
NT = (((1,), (1,)), ((), ()))
SELK, JSEL, RET, JN = 0, 12, 15, 31


def tables(pair_atoms, pair_next, z, y):
    pairs = lax.iota(jnp.int32, NZ * NY)
    same = jnp.any(pair_atoms[:, :, None, None] == pair_atoms[None, None, :, :], axis=3)
    rank = jnp.sum((same & (pairs[None, None, :] < pairs[:, None, None])).astype(jnp.int32), axis=2)
    steps = lax.iota(jnp.int32, NY)
    row_atoms = z * NY + (y + steps) % NY
    slots = lax.iota(jnp.int32, CAP)
    match = (pair_atoms[None, None] == row_atoms[:, None, None, None]) & (
        rank[None, None] == slots[None, :, None, None]
    )
    slot_pair = jnp.sum(jnp.where(match, pairs[None, None, :, None], 0), axis=(2, 3))
    selk = (z - slot_pair // NY + NZ) % NZ
    jsel = (y - slot_pair[0] % NY + NY) % NY
    code = jnp.where(
        pair_atoms // NY == z, ((y - pair_atoms % NY + NY) % NY) * CAP + rank, -1
    )
    targets = ((z + lax.iota(jnp.int32, NZ)) % NZ) * NY + y
    ret = jnp.sum(
        jnp.where(targets[:, None, None] == pairs[None, :, None], code[None], 0), axis=1
    )
    listed = pair_next[0]
    jn = (y - listed % NY + NY) % NY
    idx = (listed // (NZ * NY)) * NZ + (z - (listed % (NZ * NY)) // NY + NZ) % NZ
    tab = jnp.concatenate([selk.reshape(-1), jsel, ret.reshape(-1), jn])
    tile = jnp.pad(idx[None], ((0, 7), (0, 128 - NOV)))
    return tab, tile


def kernel(
    tab, shift, nxt, energy, b_h, c_h, f_h, s_h, i_h,
    out,
    f_v, s_v, i_v, z_b, z_c0, z_c1, n_c0, n_c1, yb_o, y_b, yc_o, y_c0, y_c1, yn_o, y_n0, y_n1, n_in, n_s,
    b_t, g_v, cc, p_v, y_t0, y_t1, bk, z_t, den, base,
    loc, zb_s, zb_r, zc_s, zc_r, nx_s, nx_r, yb_s, yb_r, yc_s, yc_r,
    fw_s, fw_r, yn_s, yn_r, yt_s, yt_r, zt_s, zt_r,
):
    z_c, n_c, y_c, y_n, y_t = (z_c0, z_c1), (n_c0, n_c1), (y_c0, y_c1), (y_n0, y_n1), (y_t0, y_t1)
    g = lax.axis_index("grp")
    d = lax.axis_index("dev")
    z, y = d // NY, d % NY
    groups = lax.axis_size("grp")
    npno = c_h.shape[1]
    kaux = f_h.shape[0]

    def at_z(k):
        return {"grp": g, "dev": ((z + k) % NZ) * NY + y}

    def at_y(j):
        return {"grp": g, "dev": z * NY + (y + j) % NY}

    before = {"grp": (g + groups - 1) % groups, "dev": d}
    after = {"grp": (g + 1) % groups, "dev": d}

    sent = []

    def send(src, dst, ss, rs, where):
        copy = pltpu.make_async_remote_copy(
            src_ref=src, dst_ref=dst, send_sem=ss, recv_sem=rs,
            device_id=where, device_id_type=MESH,
        )
        copy.start()
        sent.append(copy)
        return copy

    own = [
        pltpu.make_async_copy(f_h, f_v, loc.at[0]),
        pltpu.make_async_copy(b_h, z_b.at[0], loc.at[1]),
        pltpu.make_async_copy(c_h, z_c[0].at[0], loc.at[2]),
        pltpu.make_async_copy(s_h, s_v, loc.at[3]),
        pltpu.make_async_copy(i_h, i_v, loc.at[4]),
    ]
    for copy in own[1:]:
        copy.start()
    own[0].start()

    barrier = pltpu.get_barrier_semaphore()
    partners = [at_z(k) for k in Z_ORDER] + [at_y(j) for j in range(1, NY)] + [before, after]
    for partner in partners:
        pl.semaphore_signal(barrier, inc=1, device_id=partner, device_id_type=MESH)
    cc[...] = jnp.zeros_like(cc)
    wide = jnp.broadcast_to(energy[...], (npno, npno))
    den[...] = wide + wide.T + shift[0]
    pl.semaphore_wait(barrier, len(partners))

    zb = [send(b_h, z_b.at[k], zb_s.at[k - 1], zb_r.at[k - 1], at_z(k)) for k in Z_ORDER]
    zc = [
        send(c_h, z_c[0].at[k], zc_s.at[0, k - 1], zc_r.at[0, k - 1], at_z(k)) for k in Z_ORDER
    ]
    nx = [
        send(nxt, n_in.at[j - 1], nx_s.at[j - 1], nx_r.at[j - 1], at_y(j)) for j in range(1, NY)
    ]
    for copy in nx:
        copy.wait_recv()
    to_s = pltpu.make_async_copy(n_in, n_s, loc.at[5])
    to_s.start()
    to_s.wait()

    own[1].wait()
    for copy in zb:
        copy.wait_recv()
    yb = []
    for s in range(CAP):
        for j in range(1, NY):
            yb_o[j - 1, s] = z_b[tab[SELK + j * CAP + s]]
        for j in range(1, NY):
            yb.append(
                send(yb_o.at[j - 1, s], y_b.at[j, s], yb_s.at[j - 1, s], yb_r.at[j - 1, s], at_y(j))
            )
        y_b[0, s] = z_b[tab[SELK + s]]

    def share_amps(it, zc):
        for copy in zc:
            copy.wait_recv()
        yc = []
        for j in range(1, NY):
            for s in range(CAP):
                yc_o[it, j - 1, s] = z_c[it][tab[SELK + j * CAP + s]]
            yc.append(
                send(yc_o.at[it, j - 1], y_c[it].at[j], yc_s.at[it, j - 1], yc_r.at[it, j - 1], at_y(j))
            )
        for s in range(CAP):
            y_c[it][0, s] = z_c[it][tab[SELK + s]]
        fw = send(
            z_c[it], n_c[it].at[pl.ds(NZ, NZ)], fw_s.at[it], fw_r.at[it], before
        )
        n_c[it][:NZ] = z_c[it][...]
        return yc, fw

    def share_neighbours(it, fw):
        fw.wait_recv()
        yn = []
        for j in range(1, NY):
            for n in range(NOV):
                yn_o[it, j - 1, n] = n_c[it][n_s[NY - 1 - j, 0, n]]
            yn.append(
                send(yn_o.at[it, j - 1], y_n[it].at[j], yn_s.at[it, j - 1], yn_r.at[it, j - 1], at_y(j))
            )
        return yn

    def my_neighbour(it, n):
        return y_n[it][tab[JN + n], n]

    own[2].wait()
    yc, fw = share_amps(0, zc)
    yn = share_neighbours(0, fw)

    own[0].wait()
    for copy in yb:
        copy.wait_recv()
    for s in range(CAP):
        b_t[pl.ds(s * npno, npno), :] = y_b[tab[JSEL + s], s].T
    slot_bases = [y_b[tab[JSEL + s], s] for s in range(CAP)]

    def project(k, carry):
        half = jnp.dot(b_t[...], f_v[k], preferred_element_type=F32).astype(BF16)
        column = pl.multiple_of(k * npno, npno)
        for s in range(CAP):
            g_v[s, :, pl.ds(column, npno)] = jnp.dot(
                half[s * npno:(s + 1) * npno], slot_bases[s], preferred_element_type=F32
            ).astype(BF16)
        return carry

    lax.fori_loop(0, kaux, project, 0)
    own[3].wait()
    own[4].wait()

    for it in range(ITERS):
        for copy in yc:
            copy.wait_recv()
        yt = []
        for s in range(CAP):
            amps = y_c[it][tab[JSEL + s], s]
            cc[s, :npno, :npno] = amps
            cc[s, npno:, npno:] = amps
            for h in range(kaux // 2):
                span = pl.ds(h * 2 * npno, 2 * npno)
                p_v[s, :, span] = jnp.dot(
                    g_v[s, :, span], cc[s], preferred_element_type=F32
                ).astype(BF16)
            term = lax.dot_general(p_v[s], g_v[s], NT, preferred_element_type=F32)
            y_t[it][s] = term.astype(BF16)
            for j in range(1, NY):
                yt.append(
                    send(
                        y_t[it].at[s], y_t[it].at[j * CAP + s],
                        yt_s.at[it, j - 1, s], yt_r.at[it, j - 1, s], at_y(j),
                    )
                )
        if it > 0:
            yn = share_neighbours(it, fw)
        for copy in yt:
            copy.wait_recv()
        zt = []
        for k in (0,) + Z_ORDER:
            first, second = tab[RET + 2 * k], tab[RET + 2 * k + 1]
            total = y_t[it][jnp.maximum(first, 0)].astype(F32) * (first >= 0).astype(F32)
            total += y_t[it][jnp.maximum(second, 0)].astype(F32) * (second >= 0).astype(F32)
            if k == 0:
                base[...] = i_v[...] + total
            else:
                bk[it, k] = total.astype(BF16)
                zt.append(
                    send(bk.at[it, k], z_t.at[it, k], zt_s.at[it, k - 1], zt_r.at[it, k - 1], at_z(k))
                )
        for n in range(NOV):
            y_n[it][0, n] = n_c[it][tab[JN + NOV + n]]
        for copy in yn:
            copy.wait_recv()
        coupling = base[...]
        for n in range(NOV):
            mixed = jnp.dot(s_v[n], my_neighbour(it, n), preferred_element_type=F32).astype(BF16)
            coupling += lax.dot_general(mixed, s_v[n], NT, preferred_element_type=F32)
        base[...] = coupling
        for copy in zt:
            copy.wait_recv()
        total = base[...]
        for k in range(1, NZ):
            total += z_t[it, k].astype(F32)
        if it + 1 < ITERS:
            z_c[it + 1][0] = (-total / den[...]).astype(BF16)
            zc = [
                send(
                    z_c[it + 1].at[0], z_c[it + 1].at[k],
                    zc_s.at[it + 1, k - 1], zc_r.at[it + 1, k - 1], at_z(k),
                )
                for k in Z_ORDER
            ]
            yc, fw = share_amps(it + 1, zc)
        else:
            out[...] = total
    for copy in sent:
        copy.wait_send()


def on_device(
    amplitudes,
    bases,
    factors,
    intersections,
    pair_integrals,
    pno_energies,
    pair_shift,
    pair_atoms,
    pair_next,
):
    d = lax.axis_index("dev")
    z, y = d // NY, d % NY
    tab, tile = tables(pair_atoms, pair_next, z, y)
    tab = jnp.concatenate([tab, tile[0, :NOV]])
    npno, npao, kaux = amplitudes.shape[1], bases.shape[1], factors.shape[1]
    vm = pltpu.VMEM
    dma = pltpu.SemaphoreType.DMA
    smem = pl.BlockSpec(memory_space=pltpu.SMEM)
    vmem = pl.BlockSpec(memory_space=pltpu.VMEM)
    hbm = pl.BlockSpec(memory_space=pl.ANY)
    total = pl.pallas_call(
        kernel,
        out_shape=jax.ShapeDtypeStruct((npno, npno), F32),
        in_specs=[smem, smem, vmem, vmem, hbm, hbm, hbm, hbm, hbm],
        out_specs=vmem,
        scratch_shapes=[
            vm((kaux, npao, npao), BF16),
            vm((NOV, npno, npno), BF16),
            vm((npno, npno), F32),
            vm((NZ, npao, npno), BF16),
            vm((NZ, npno, npno), BF16),
            vm((NZ, npno, npno), BF16),
            vm((2 * NZ, npno, npno), BF16),
            vm((2 * NZ, npno, npno), BF16),
            vm((NY - 1, CAP, npao, npno), BF16),
            vm((NY, CAP, npao, npno), BF16),
            vm((ITERS, NY - 1, CAP, npno, npno), BF16),
            vm((NY, CAP, npno, npno), BF16),
            vm((NY, CAP, npno, npno), BF16),
            vm((ITERS, NY - 1, NOV, npno, npno), BF16),
            vm((NY, NOV, npno, npno), BF16),
            vm((NY, NOV, npno, npno), BF16),
            vm((NY - 1, 8, 128), jnp.int32),
            pltpu.SMEM((NY - 1, 8, 128), jnp.int32),
            vm((CAP * npno, npao), BF16),
            vm((CAP, npno, kaux * npno), BF16),
            vm((CAP, 2 * npno, 2 * npno), BF16),
            vm((CAP, npno, kaux * npno), BF16),
            vm((NY * CAP, npno, npno), BF16),
            vm((NY * CAP, npno, npno), BF16),
            vm((ITERS, NZ, npno, npno), BF16),
            vm((ITERS, NZ, npno, npno), BF16),
            vm((npno, npno), F32),
            vm((npno, npno), F32),
            dma((6,)),
            dma((NZ - 1,)),
            dma((NZ - 1,)),
            dma((ITERS, NZ - 1)),
            dma((ITERS, NZ - 1)),
            dma((NY - 1,)),
            dma((NY - 1,)),
            dma((NY - 1, CAP)),
            dma((NY - 1, CAP)),
            dma((ITERS, NY - 1)),
            dma((ITERS, NY - 1)),
            dma((ITERS,)),
            dma((ITERS,)),
            dma((ITERS, NY - 1)),
            dma((ITERS, NY - 1)),
            dma((ITERS, NY - 1, CAP)),
            dma((ITERS, NY - 1, CAP)),
            dma((ITERS, NZ - 1)),
            dma((ITERS, NZ - 1)),
        ],
        compiler_params=pltpu.CompilerParams(
            collective_id=0, has_side_effects=True, vmem_limit_bytes=48 << 20
        ),
        name="ladder",
    )(
        tab, pair_shift, tile, pno_energies, bases[0], amplitudes[0], factors[0],
        intersections[0], pair_integrals[0],
    )
    denominator = pno_energies[0][:, None] + pno_energies[0][None, :] + pair_shift[0]
    return (-total / denominator)[None]


def solution(mesh):
    return jax.shard_map(
        on_device,
        mesh=mesh,
        in_specs=(
            P(("grp", "dev"), None, None),
            P(("grp", "dev"), None, None),
            P(("grp", "dev"), None, None, None),
            P(("grp", "dev"), None, None, None),
            P(("grp", "dev"), None, None),
            P(("grp", "dev"), None),
            P(("grp", "dev")),
            P("grp", None),
            P(("grp", "dev"), None),
        ),
        out_specs=P(("grp", "dev"), None, None),
        check_vma=False,
    )
```

```python
import jax
import jax.numpy as jnp
from jax import lax
from jax.experimental import pallas as pl
from jax.experimental.pallas import tpu as pltpu
from jax.sharding import PartitionSpec as P

CAP = 3
ITERS = 2
NZ = 8
NY = 4
NOV = 4
BATCH = 4
F32 = jnp.float32
BF16 = jnp.bfloat16
MESH = pl.DeviceIdType.MESH
Z_ORDER = (4, 3, 5, 2, 6, 1, 7)
NT = (((1,), (1,)), ((), ()))
PAIR, SELK, JSEL, RET, TAB = 0, 12, 24, 27, 43


def scan_pairs(pa_s, tab, z, y):
    def visit(p, carry):
        counts, found = carry
        counts, found = list(counts), list(found)
        for j in range(NY):
            atom = z * NY + ((y + j) & (NY - 1))
            hit = (pa_s[0, p] == atom) | (pa_s[1, p] == atom)
            for s in range(CAP):
                found[j * CAP + s] = jnp.where(
                    hit & (counts[j] == s), p, found[j * CAP + s]
                )
            counts[j] = counts[j] + hit.astype(jnp.int32)
        return tuple(counts), tuple(found)

    zero, none = jnp.int32(0), jnp.int32(-1)
    _, found = lax.fori_loop(0, NZ * NY, visit, ((zero,) * NY, (none,) * (NY * CAP)))
    for i in range(NY * CAP):
        pair = jnp.maximum(found[i], 0)
        tab[PAIR + i] = found[i]
        tab[SELK + i] = (z - (pair >> 2)) & (NZ - 1)
        if i < CAP:
            tab[JSEL + i] = (y - (pair & (NY - 1))) & (NY - 1)
    for k in range(NZ):
        pair = ((z + k) & (NZ - 1)) * NY + y
        for i in range(2):
            atom = pa_s[i, pair]
            j = (y - (atom & (NY - 1))) & (NY - 1)
            mate = ((NY - j) & (NY - 1)) * CAP
            rank = jnp.where(tab[PAIR + mate + 1] == pair, 1, 0) + jnp.where(
                tab[PAIR + mate + 2] == pair, 2, 0
            )
            tab[RET + 2 * k + i] = jnp.where((atom >> 2) == z, j * CAP + rank, -1)


def kernel(
    pa_h, pn_h, sh_h, e_h, b_h, c_h, f_h, s_h, i_h,
    out,
    pa_s, pn_s, sh_s, e_v, tab, f_v, s_v, i_v, z_b, z_c0, z_c1, n_c0, n_c1, yb_o, y_b, yc_o, y_c0, y_c1, yn_o, y_n0, y_n1, n_in, n_s,
    b_t, y_s, g_v, cc, p_v, y_t0, y_t1, bk, z_t, den, base,
    loc, zb_s, zb_r, zc_s, zc_r, nx_s, nx_r, yb_s, yb_r, yc_s, yc_r,
    fw_s, fw_r, yn_s, yn_r, yt_s, yt_r, zt_s, zt_r,
):
    z_c, n_c, y_c, y_n, y_t = (z_c0, z_c1), (n_c0, n_c1), (y_c0, y_c1), (y_n0, y_n1), (y_t0, y_t1)
    g = lax.axis_index("grp")
    d = lax.axis_index("dev")
    z, y = d // NY, d % NY
    groups = lax.axis_size("grp")
    npno = c_h.shape[1]
    kaux = f_h.shape[0]

    def at_z(k):
        return {"grp": g, "dev": ((z + k) % NZ) * NY + y}

    def at_y(j):
        return {"grp": g, "dev": z * NY + (y + j) % NY}

    before = {"grp": (g + groups - 1) % groups, "dev": d}
    after = {"grp": (g + 1) % groups, "dev": d}

    sent = []

    def send(src, dst, ss, rs, where):
        copy = pltpu.make_async_remote_copy(
            src_ref=src, dst_ref=dst, send_sem=ss, recv_sem=rs,
            device_id=where, device_id_type=MESH,
        )
        copy.start()
        sent.append(copy)
        return copy

    own = [
        pltpu.make_async_copy(f_h, f_v, loc.at[0]),
        pltpu.make_async_copy(b_h, z_b.at[0], loc.at[1]),
        pltpu.make_async_copy(c_h, z_c[0].at[0], loc.at[2]),
        pltpu.make_async_copy(s_h, s_v, loc.at[3]),
        pltpu.make_async_copy(i_h, i_v, loc.at[4]),
    ]
    small = [
        pltpu.make_async_copy(pa_h, pa_s, loc.at[6]),
        pltpu.make_async_copy(pn_h, pn_s, loc.at[7]),
        pltpu.make_async_copy(sh_h, sh_s, loc.at[8]),
        pltpu.make_async_copy(e_h, e_v, loc.at[9]),
    ]
    for copy in small:
        copy.start()
    for copy in own[1:]:
        copy.start()
    own[0].start()

    barrier = pltpu.get_barrier_semaphore()
    partners = [at_z(k) for k in Z_ORDER] + [at_y(j) for j in range(1, NY)] + [before, after]
    for partner in partners:
        pl.semaphore_signal(barrier, inc=1, device_id=partner, device_id_type=MESH)
    cc[...] = jnp.zeros_like(cc)
    for copy in small:
        copy.wait()
    scan_pairs(pa_s, tab, z, y)
    pl.semaphore_wait(barrier, len(partners))

    zb = [send(b_h, z_b.at[k], zb_s.at[k - 1], zb_r.at[k - 1], at_z(k)) for k in Z_ORDER]
    zc = [
        send(c_h, z_c[0].at[k], zc_s.at[0, k - 1], zc_r.at[0, k - 1], at_z(k)) for k in Z_ORDER
    ]
    nx = [
        send(pn_h, n_in.at[j - 1], nx_s.at[j - 1], nx_r.at[j - 1], at_y(j)) for j in range(1, NY)
    ]
    for copy in nx:
        copy.wait_recv()
    to_s = pltpu.make_async_copy(n_in, n_s, loc.at[5])
    to_s.start()
    to_s.wait()

    wide = jnp.broadcast_to(e_v[...], (npno, npno))
    den[...] = wide + wide.T + sh_s[0]
    own[1].wait()
    for copy in zb:
        copy.wait_recv()
    yb = []
    for s in range(CAP):
        for j in range(1, NY):
            yb_o[j - 1, s] = z_b[tab[SELK + j * CAP + s]]
        for j in range(1, NY):
            yb.append(
                send(yb_o.at[j - 1, s], y_b.at[j, s], yb_s.at[j - 1, s], yb_r.at[j - 1, s], at_y(j))
            )
        y_b[0, s] = z_b[tab[SELK + s]]

    def share_amps(it, zc):
        for copy in zc:
            copy.wait_recv()
        yc = []
        for j in range(1, NY):
            for s in range(CAP):
                yc_o[it, j - 1, s] = z_c[it][tab[SELK + j * CAP + s]]
            yc.append(
                send(yc_o.at[it, j - 1], y_c[it].at[j], yc_s.at[it, j - 1], yc_r.at[it, j - 1], at_y(j))
            )
        for s in range(CAP):
            y_c[it][0, s] = z_c[it][tab[SELK + s]]
        fw = send(
            z_c[it], n_c[it].at[pl.ds(NZ, NZ)], fw_s.at[it], fw_r.at[it], before
        )
        n_c[it][:NZ] = z_c[it][...]
        return yc, fw

    def share_neighbours(it, fw):
        fw.wait_recv()
        yn = []
        for j in range(1, NY):
            for n in range(NOV):
                listed = n_s[NY - 1 - j, 0, n]
                yn_o[it, j - 1, n] = n_c[it][(listed >> 5) * NZ + ((z - ((listed & 31) >> 2)) & (NZ - 1))]
            yn.append(
                send(yn_o.at[it, j - 1], y_n[it].at[j], yn_s.at[it, j - 1], yn_r.at[it, j - 1], at_y(j))
            )
        return yn

    def my_neighbour(it, n):
        return y_n[it][(y - (pn_s[0, n] & (NY - 1))) & (NY - 1), n]

    own[2].wait()
    yc, fw = share_amps(0, zc)
    yn = share_neighbours(0, fw)

    own[0].wait()
    for copy in yb:
        copy.wait_recv()
    for s in range(CAP):
        b_t[pl.ds(s * npno, npno), :] = y_b[tab[JSEL + s], s].T
    def project(kk, carry):
        for u in range(BATCH):
            half = jnp.dot(b_t[...], f_v[kk * BATCH + u], preferred_element_type=F32).astype(BF16)
            for s in range(CAP):
                y_s[s, u * npno:(u + 1) * npno] = half[s * npno:(s + 1) * npno]
        column = pl.multiple_of(kk * (npno * BATCH), npno * BATCH)
        for s in range(CAP):
            inner = jnp.dot(
                y_s[s], y_b[tab[JSEL + s], s], preferred_element_type=F32
            ).astype(BF16)
            for u in range(BATCH):
                g_v[s, :, pl.ds(column + u * npno, npno)] = inner[u * npno:(u + 1) * npno]
        return carry

    lax.fori_loop(0, kaux // BATCH, project, 0)
    own[3].wait()
    own[4].wait()

    for it in range(ITERS):
        for copy in yc:
            copy.wait_recv()
        yt = []
        for s in range(CAP):
            amps = y_c[it][tab[JSEL + s], s]
            cc[s, :npno, :npno] = amps
            cc[s, npno:, npno:] = amps
            for h in range(kaux // 2):
                span = pl.ds(h * 2 * npno, 2 * npno)
                p_v[s, :, span] = jnp.dot(
                    g_v[s, :, span], cc[s], preferred_element_type=F32
                ).astype(BF16)
            term = lax.dot_general(p_v[s], g_v[s], NT, preferred_element_type=F32)
            y_t[it][s] = term.astype(BF16)
            for j in range(1, NY):
                yt.append(
                    send(
                        y_t[it].at[s], y_t[it].at[j * CAP + s],
                        yt_s.at[it, j - 1, s], yt_r.at[it, j - 1, s], at_y(j),
                    )
                )
        if it > 0:
            yn = share_neighbours(it, fw)
        for copy in yt:
            copy.wait_recv()
        zt = []
        for k in (0,) + Z_ORDER:
            first, second = tab[RET + 2 * k], tab[RET + 2 * k + 1]
            total = y_t[it][jnp.maximum(first, 0)].astype(F32) * (first >= 0).astype(F32)
            total += y_t[it][jnp.maximum(second, 0)].astype(F32) * (second >= 0).astype(F32)
            if k == 0:
                base[...] = i_v[...] + total
            else:
                bk[it, k] = total.astype(BF16)
                zt.append(
                    send(bk.at[it, k], z_t.at[it, k], zt_s.at[it, k - 1], zt_r.at[it, k - 1], at_z(k))
                )
        for n in range(NOV):
            listed = pn_s[0, n]
            y_n[it][0, n] = n_c[it][(listed >> 5) * NZ + ((z - ((listed & 31) >> 2)) & (NZ - 1))]
        for copy in yn:
            copy.wait_recv()
        coupling = base[...]
        for n in range(NOV):
            mixed = jnp.dot(s_v[n], my_neighbour(it, n), preferred_element_type=F32).astype(BF16)
            coupling += lax.dot_general(mixed, s_v[n], NT, preferred_element_type=F32)
        base[...] = coupling
        for copy in zt:
            copy.wait_recv()
        total = base[...]
        for k in range(1, NZ):
            total += z_t[it, k].astype(F32)
        if it + 1 < ITERS:
            z_c[it + 1][0] = (-total / den[...]).astype(BF16)
            zc = [
                send(
                    z_c[it + 1].at[0], z_c[it + 1].at[k],
                    zc_s.at[it + 1, k - 1], zc_r.at[it + 1, k - 1], at_z(k),
                )
                for k in Z_ORDER
            ]
            yc, fw = share_amps(it + 1, zc)
        else:
            out[...] = total
    for copy in sent:
        copy.wait_send()


def on_device(
    amplitudes,
    bases,
    factors,
    intersections,
    pair_integrals,
    pno_energies,
    pair_shift,
    pair_atoms,
    pair_next,
):
    npno, npao, kaux = amplitudes.shape[1], bases.shape[1], factors.shape[1]
    vm = pltpu.VMEM
    dma = pltpu.SemaphoreType.DMA
    vmem = pl.BlockSpec(memory_space=pltpu.VMEM)
    hbm = pl.BlockSpec(memory_space=pl.ANY)
    total = pl.pallas_call(
        kernel,
        out_shape=jax.ShapeDtypeStruct((npno, npno), F32),
        in_specs=[hbm] * 9,
        out_specs=vmem,
        scratch_shapes=[
            pltpu.SMEM(pair_atoms.shape[::-1], jnp.int32),
            pltpu.SMEM(pair_next.shape, jnp.int32),
            pltpu.SMEM((1,), F32),
            vm((1, npno), F32),
            pltpu.SMEM((TAB,), jnp.int32),
            vm((kaux, npao, npao), BF16),
            vm((NOV, npno, npno), BF16),
            vm((npno, npno), F32),
            vm((NZ, npao, npno), BF16),
            vm((NZ, npno, npno), BF16),
            vm((NZ, npno, npno), BF16),
            vm((2 * NZ, npno, npno), BF16),
            vm((2 * NZ, npno, npno), BF16),
            vm((NY - 1, CAP, npao, npno), BF16),
            vm((NY, CAP, npao, npno), BF16),
            vm((ITERS, NY - 1, CAP, npno, npno), BF16),
            vm((NY, CAP, npno, npno), BF16),
            vm((NY, CAP, npno, npno), BF16),
            vm((ITERS, NY - 1, NOV, npno, npno), BF16),
            vm((NY, NOV, npno, npno), BF16),
            vm((NY, NOV, npno, npno), BF16),
            vm((NY - 1, 1, NOV), jnp.int32),
            pltpu.SMEM((NY - 1, 1, NOV), jnp.int32),
            vm((CAP * npno, npao), BF16),
            vm((CAP, BATCH * npno, npao), BF16),
            vm((CAP, npno, kaux * npno), BF16),
            vm((CAP, 2 * npno, 2 * npno), BF16),
            vm((CAP, npno, kaux * npno), BF16),
            vm((NY * CAP, npno, npno), BF16),
            vm((NY * CAP, npno, npno), BF16),
            vm((ITERS, NZ, npno, npno), BF16),
            vm((ITERS, NZ, npno, npno), BF16),
            vm((npno, npno), F32),
            vm((npno, npno), F32),
            dma((10,)),
            dma((NZ - 1,)),
            dma((NZ - 1,)),
            dma((ITERS, NZ - 1)),
            dma((ITERS, NZ - 1)),
            dma((NY - 1,)),
            dma((NY - 1,)),
            dma((NY - 1, CAP)),
            dma((NY - 1, CAP)),
            dma((ITERS, NY - 1)),
            dma((ITERS, NY - 1)),
            dma((ITERS,)),
            dma((ITERS,)),
            dma((ITERS, NY - 1)),
            dma((ITERS, NY - 1)),
            dma((ITERS, NY - 1, CAP)),
            dma((ITERS, NY - 1, CAP)),
            dma((ITERS, NZ - 1)),
            dma((ITERS, NZ - 1)),
        ],
        compiler_params=pltpu.CompilerParams(
            collective_id=0, has_side_effects=True, vmem_limit_bytes=67043328
        ),
        name="ladder",
    )(
        pair_atoms.T, pair_next, pair_shift, pno_energies, bases[0], amplitudes[0], factors[0],
        intersections[0], pair_integrals[0],
    )
    denominator = pno_energies[0][:, None] + pno_energies[0][None, :] + pair_shift[0]
    return (-total / denominator)[None]


def solution(mesh):
    return jax.shard_map(
        on_device,
        mesh=mesh,
        in_specs=(
            P(("grp", "dev"), None, None),
            P(("grp", "dev"), None, None),
            P(("grp", "dev"), None, None, None),
            P(("grp", "dev"), None, None, None),
            P(("grp", "dev"), None, None),
            P(("grp", "dev"), None),
            P(("grp", "dev")),
            P("grp", None),
            P(("grp", "dev"), None),
        ),
        out_specs=P(("grp", "dev"), None, None),
        check_vma=False,
    )
```

```python
import jax
import jax.numpy as jnp
from jax import lax
from jax.experimental import pallas as pl
from jax.experimental.pallas import tpu as pltpu
from jax.sharding import PartitionSpec as P

CAP = 3
ITERS = 2
NZ = 8
NY = 4
NOV = 4
BATCH = 4
CHUNKS = 4
EARLY = 3
F32 = jnp.float32
BF16 = jnp.bfloat16
MESH = pl.DeviceIdType.MESH
Z_ORDER = (4, 3, 5, 2, 6, 1, 7)
NT = (((1,), (1,)), ((), ()))
PAIR, SELK, JSEL, RET, TAB = 0, 12, 24, 27, 43


def scan_pairs(pa_s, tab, z, y):
    def visit(p, carry):
        counts, found = carry
        counts, found = list(counts), list(found)
        for j in range(NY):
            atom = z * NY + ((y + j) & (NY - 1))
            hit = (pa_s[0, p] == atom) | (pa_s[1, p] == atom)
            for s in range(CAP):
                found[j * CAP + s] = jnp.where(hit & (counts[j] == s), p, found[j * CAP + s])
            counts[j] = counts[j] + hit.astype(jnp.int32)
        return tuple(counts), tuple(found)

    zero, none = jnp.int32(0), jnp.int32(-1)
    _, found = lax.fori_loop(0, NZ * NY, visit, ((zero,) * NY, (none,) * (NY * CAP)))
    for i in range(NY * CAP):
        pair = jnp.maximum(found[i], 0)
        tab[PAIR + i] = found[i]
        tab[SELK + i] = (z - (pair >> 2)) & (NZ - 1)
        if i < CAP:
            tab[JSEL + i] = (y - (pair & (NY - 1))) & (NY - 1)
    for k in range(NZ):
        pair = ((z + k) & (NZ - 1)) * NY + y
        for i in range(2):
            atom = pa_s[i, pair]
            j = (y - (atom & (NY - 1))) & (NY - 1)
            mate = ((NY - j) & (NY - 1)) * CAP
            rank = jnp.where(tab[PAIR + mate + 1] == pair, 1, 0) + jnp.where(
                tab[PAIR + mate + 2] == pair, 2, 0
            )
            tab[RET + 2 * k + i] = jnp.where((atom >> 2) == z, j * CAP + rank, -1)


def scratch(npno, npao, kaux):
    vm, dma, sm = pltpu.VMEM, pltpu.SemaphoreType.DMA, pltpu.SMEM
    rows = npno // CHUNKS
    square = (npno, npno)
    shapes = {
        "pa_s": sm((2, NZ * NY), jnp.int32),
        "pn_s": sm((1, NOV), jnp.int32),
        "sh_s": sm((1,), F32),
        "e_v": vm((1, npno), F32),
        "tab": sm((TAB,), jnp.int32),
        "f_v": vm((kaux, npao, npao), BF16),
        "s_v": vm((NOV,) + square, BF16),
        "i_v": vm(square, F32),
        "b_v": vm((npao, npno), BF16),
        "n_in": vm((NY - 1, 1, NOV), jnp.int32),
        "n_s": sm((NY - 1, 1, NOV), jnp.int32),
        "lhs_a": vm((CAP * EARLY * rows, npao), BF16),
        "lhs_b": vm((CAP * (CHUNKS - EARLY) * rows, npao), BF16),
        "b_t": vm((CAP, npno, npao), BF16),
        "half": vm((CAP, kaux * npno, npao), BF16),
        "g_v": vm((CAP, npno, kaux * npno), BF16),
        "p_v": vm((CAP, npno, kaux * npno), BF16),
        "cc": vm((CAP, 2 * npno, 2 * npno), BF16),
        "den": vm(square, F32),
        "base": vm(square, F32),
        "loc": dma((10,)),
        "nx": (dma((NY - 1,)), dma((NY - 1,))),
    }
    for c in range(CHUNKS):
        shapes[f"zb{c}"] = vm((NZ, rows, npao), BF16)
        shapes[f"ybo{c}"] = vm((NY - 1, CAP, rows, npao), BF16)
        shapes[f"yb{c}"] = vm((NY, CAP, rows, npao), BF16)
    shapes["zb"] = (dma((CHUNKS, NZ - 1)), dma((CHUNKS, NZ - 1)))
    shapes["yb"] = (dma((CHUNKS, NY - 1)), dma((CHUNKS, NY - 1)))
    for it in range(ITERS):
        shapes[f"zc{it}"] = vm((NZ,) + square, BF16)
        shapes[f"nc{it}"] = vm((2 * NZ,) + square, BF16)
        for s in range(CAP):
            shapes[f"yc{it}{s}"] = vm((NY,) + square, BF16)
        shapes[f"yco{it}"] = vm((CAP, NY - 1) + square, BF16)
        shapes[f"yn{it}"] = vm((NY, NOV) + square, BF16)
        shapes[f"yno{it}"] = vm((NY - 1, NOV) + square, BF16)
        shapes[f"yt{it}"] = vm((NY * CAP,) + square, BF16)
        shapes[f"bk{it}"] = vm((NZ,) + square, BF16)
        shapes[f"zt{it}"] = vm((NZ,) + square, BF16)
    shapes["zc"] = (dma((ITERS, NZ - 1)), dma((ITERS, NZ - 1)))
    shapes["yc"] = (dma((ITERS, CAP, NY - 1)), dma((ITERS, CAP, NY - 1)))
    shapes["fw"] = (dma((ITERS,)), dma((ITERS,)))
    shapes["yn"] = (dma((ITERS, NY - 1)), dma((ITERS, NY - 1)))
    shapes["yt"] = (dma((ITERS, CAP, NY - 1)), dma((ITERS, CAP, NY - 1)))
    shapes["zt"] = (dma((ITERS, NZ - 1)), dma((ITERS, NZ - 1)))
    flat = {}
    for name, shape in shapes.items():
        if isinstance(shape, tuple):
            flat[name + "_s"], flat[name + "_r"] = shape
        else:
            flat[name] = shape
    return flat


def kernel(names, pa_h, pn_h, sh_h, e_h, b_h, c_h, f_h, s_h, i_h, out, *refs):
    r = dict(zip(names, refs))
    tab, loc, half, g_v, p_v, cc = r["tab"], r["loc"], r["half"], r["g_v"], r["p_v"], r["cc"]
    g = lax.axis_index("grp")
    d = lax.axis_index("dev")
    z, y = d // NY, d % NY
    groups = lax.axis_size("grp")
    npno = c_h.shape[1]
    kaux = f_h.shape[0]
    rows = npno // CHUNKS

    def at_z(k):
        return {"grp": g, "dev": ((z + k) % NZ) * NY + y}

    def at_y(j):
        return {"grp": g, "dev": z * NY + (y + j) % NY}

    before = {"grp": (g + groups - 1) % groups, "dev": d}
    after = {"grp": (g + 1) % groups, "dev": d}

    sent = []

    def send(src, dst, name, index, where):
        copy = pltpu.make_async_remote_copy(
            src_ref=src, dst_ref=dst,
            send_sem=r[name + "_s"].at[index], recv_sem=r[name + "_r"].at[index],
            device_id=where, device_id_type=MESH,
        )
        copy.start()
        sent.append(copy)
        return copy

    def arrive(copies):
        for copy in copies:
            copy.wait_recv()

    def local(src, dst, number):
        copy = pltpu.make_async_copy(src, dst, loc.at[number])
        copy.start()
        return copy

    own_b = local(b_h, r["b_v"], 0)
    small = [
        local(pa_h, r["pa_s"], 1),
        local(pn_h, r["pn_s"], 2),
        local(sh_h, r["sh_s"], 3),
        local(e_h, r["e_v"], 4),
    ]
    own_c = local(c_h, r["zc0"].at[0], 5)
    own_f = local(f_h, r["f_v"], 6)
    own_s = local(s_h, r["s_v"], 7)
    own_i = local(i_h, r["i_v"], 8)

    barrier = pltpu.get_barrier_semaphore()
    partners = [at_z(k) for k in Z_ORDER] + [at_y(j) for j in range(1, NY)] + [before, after]
    for partner in partners:
        pl.semaphore_signal(barrier, inc=1, device_id=partner, device_id_type=MESH)
    cc[...] = jnp.zeros_like(cc)
    own_b.wait()
    flipped = r["b_v"][...].T
    for c in range(CHUNKS):
        r[f"zb{c}"][0] = flipped[c * rows:(c + 1) * rows]
    for copy in small:
        copy.wait()
    scan_pairs(r["pa_s"], tab, z, y)
    wide = jnp.broadcast_to(r["e_v"][...], (npno, npno))
    r["den"][...] = wide + wide.T + r["sh_s"][0]
    own_c.wait()
    pl.semaphore_wait(barrier, len(partners))

    zb = [
        [send(r[f"zb{c}"].at[0], r[f"zb{c}"].at[k], "zb", (c, k - 1), at_z(k)) for k in Z_ORDER]
        for c in range(CHUNKS)
    ]
    zc = [send(c_h, r["zc0"].at[k], "zc", (0, k - 1), at_z(k)) for k in Z_ORDER]
    nx = [send(pn_h, r["n_in"].at[j - 1], "nx", j - 1, at_y(j)) for j in range(1, NY)]

    yb = []
    for c in range(CHUNKS):
        arrive(zb[c])
        for j in range(1, NY):
            for s in range(CAP):
                r[f"ybo{c}"][j - 1, s] = r[f"zb{c}"][tab[SELK + j * CAP + s]]
            yb.append(
                send(r[f"ybo{c}"].at[j - 1], r[f"yb{c}"].at[j], "yb", (c, j - 1), at_y(j))
            )
        for s in range(CAP):
            r[f"yb{c}"][0, s] = r[f"zb{c}"][tab[SELK + s]]

    def collect(first, last, lhs):
        height = (last - first) * rows
        for s in range(CAP):
            for c in range(first, last):
                block = r[f"yb{c}"][tab[JSEL + s], s]
                lhs[pl.ds(s * height + (c - first) * rows, rows), :] = block
                r["b_t"][s, pl.ds(c * rows, rows), :] = block

    def first_product(first, last, lhs):
        height = (last - first) * rows

        def step(kk, carry):
            for u in range(BATCH):
                part = jnp.dot(
                    lhs[...], r["f_v"][kk * BATCH + u], preferred_element_type=F32
                ).astype(BF16)
                start = pl.multiple_of(kk * (npno * BATCH), npno * BATCH)
                for s in range(CAP):
                    half[s, pl.ds(start + u * npno + first * rows, height), :] = part[
                        s * height:(s + 1) * height
                    ]
            return carry

        lax.fori_loop(0, kaux // BATCH, step, 0)

    def share_amps(it, zc):
        arrive(zc)
        yc = []
        for s in range(CAP):
            for j in range(1, NY):
                r[f"yco{it}"][s, j - 1] = r[f"zc{it}"][tab[SELK + j * CAP + s]]
            yc.append([
                send(
                    r[f"yco{it}"].at[s, j - 1], r[f"yc{it}{s}"].at[j], "yc", (it, s, j - 1), at_y(j)
                )
                for j in range(1, NY)
            ])
            r[f"yc{it}{s}"][0] = r[f"zc{it}"][tab[SELK + s]]
        fw = send(r[f"zc{it}"], r[f"nc{it}"].at[pl.ds(NZ, NZ)], "fw", it, before)
        r[f"nc{it}"][:NZ] = r[f"zc{it}"][...]
        return yc, fw

    def place(listed):
        return (listed >> 5) * NZ + ((z - ((listed & 31) >> 2)) & (NZ - 1))

    def share_neighbours(it, fw):
        fw.wait_recv()
        yn = []
        for j in range(1, NY):
            for n in range(NOV):
                r[f"yno{it}"][j - 1, n] = r[f"nc{it}"][place(r["n_s"][NY - 1 - j, 0, n])]
            yn.append(
                send(r[f"yno{it}"].at[j - 1], r[f"yn{it}"].at[j], "yn", (it, j - 1), at_y(j))
            )
        for n in range(NOV):
            r[f"yn{it}"][0, n] = r[f"nc{it}"][place(r["pn_s"][0, n])]
        return yn

    arrive(nx)
    to_s = local(r["n_in"], r["n_s"], 9)
    own_f.wait()
    arrive(yb[:EARLY * (NY - 1)])
    collect(0, EARLY, r["lhs_a"])
    first_product(0, EARLY, r["lhs_a"])
    yc, fw = share_amps(0, zc)
    arrive(yb[EARLY * (NY - 1):])
    collect(EARLY, CHUNKS, r["lhs_b"])
    first_product(EARLY, CHUNKS, r["lhs_b"])

    def second_product(kk, carry):
        start = pl.multiple_of(kk * (npno * BATCH), npno * BATCH)
        for s in range(CAP):
            inner = lax.dot_general(
                half[s, pl.ds(start, npno * BATCH), :], r["b_t"][s], NT,
                preferred_element_type=F32,
            ).astype(BF16)
            for u in range(BATCH):
                g_v[s, :, pl.ds(start + u * npno, npno)] = inner[u * npno:(u + 1) * npno]
        return carry

    lax.fori_loop(0, kaux // BATCH, second_product, 0)
    to_s.wait()
    own_s.wait()
    own_i.wait()

    for it in range(ITERS):
        yt = []
        for s in range(CAP):
            arrive(yc[s])
            amps = r[f"yc{it}{s}"][tab[JSEL + s]]
            cc[s, :npno, :npno] = amps
            cc[s, npno:, npno:] = amps
            for h in range(kaux // 2):
                span = pl.ds(h * 2 * npno, 2 * npno)
                p_v[s, :, span] = jnp.dot(
                    g_v[s, :, span], cc[s], preferred_element_type=F32
                ).astype(BF16)
            term = lax.dot_general(p_v[s], g_v[s], NT, preferred_element_type=F32)
            r[f"yt{it}"][s] = term.astype(BF16)
            for j in range(1, NY):
                yt.append(
                    send(
                        r[f"yt{it}"].at[s], r[f"yt{it}"].at[j * CAP + s],
                        "yt", (it, s, j - 1), at_y(j),
                    )
                )
        yn = share_neighbours(it, fw)
        arrive(yt)
        zt = []
        for k in (0,) + Z_ORDER:
            total = jnp.zeros((npno, npno), F32)
            for i in range(2):
                slot = tab[RET + 2 * k + i]
                weight = (slot >= 0).astype(F32)
                total += r[f"yt{it}"][jnp.maximum(slot, 0)].astype(F32) * weight
            if k == 0:
                r["base"][...] = r["i_v"][...] + total
            else:
                r[f"bk{it}"][k] = total.astype(BF16)
                zt.append(
                    send(r[f"bk{it}"].at[k], r[f"zt{it}"].at[k], "zt", (it, k - 1), at_z(k))
                )
        arrive(yn)
        coupling = r["base"][...]
        for n in range(NOV):
            other = r[f"yn{it}"][(y - (r["pn_s"][0, n] & (NY - 1))) & (NY - 1), n]
            mixed = jnp.dot(r["s_v"][n], other, preferred_element_type=F32).astype(BF16)
            coupling += lax.dot_general(mixed, r["s_v"][n], NT, preferred_element_type=F32)
        r["base"][...] = coupling
        arrive(zt)
        total = r["base"][...]
        for k in range(1, NZ):
            total += r[f"zt{it}"][k].astype(F32)
        if it + 1 < ITERS:
            column = r[f"zc{it + 1}"]
            column[0] = (-total / r["den"][...]).astype(BF16)
            zc = [
                send(column.at[0], column.at[k], "zc", (it + 1, k - 1), at_z(k)) for k in Z_ORDER
            ]
            yc, fw = share_amps(it + 1, zc)
        else:
            out[...] = total
    for copy in sent:
        copy.wait_send()


def on_device(
    amplitudes,
    bases,
    factors,
    intersections,
    pair_integrals,
    pno_energies,
    pair_shift,
    pair_atoms,
    pair_next,
):
    npno, npao, kaux = amplitudes.shape[1], bases.shape[1], factors.shape[1]
    shapes = scratch(npno, npao, kaux)
    names = tuple(shapes)

    def body(*refs):
        kernel(names, *refs)

    total = pl.pallas_call(
        body,
        out_shape=jax.ShapeDtypeStruct((npno, npno), F32),
        in_specs=[pl.BlockSpec(memory_space=pl.ANY)] * 9,
        out_specs=pl.BlockSpec(memory_space=pltpu.VMEM),
        scratch_shapes=list(shapes.values()),
        compiler_params=pltpu.CompilerParams(
            collective_id=0, has_side_effects=True, vmem_limit_bytes=67043328
        ),
        name="ladder",
    )(
        pair_atoms.T, pair_next, pair_shift, pno_energies, bases[0], amplitudes[0], factors[0],
        intersections[0], pair_integrals[0],
    )
    denominator = pno_energies[0][:, None] + pno_energies[0][None, :] + pair_shift[0]
    return (-total / denominator)[None]


def solution(mesh):
    return jax.shard_map(
        on_device,
        mesh=mesh,
        in_specs=(
            P(("grp", "dev"), None, None),
            P(("grp", "dev"), None, None),
            P(("grp", "dev"), None, None, None),
            P(("grp", "dev"), None, None, None),
            P(("grp", "dev"), None, None),
            P(("grp", "dev"), None),
            P(("grp", "dev")),
            P("grp", None),
            P(("grp", "dev"), None),
        ),
        out_specs=P(("grp", "dev"), None, None),
        check_vma=False,
    )
```

```python
import jax
import jax.numpy as jnp
from jax import lax
from jax.experimental import pallas as pl
from jax.experimental.pallas import tpu as pltpu
from jax.sharding import PartitionSpec as P

CAP = 3
ITERS = 2
NZ = 8
NY = 4
NOV = 4
BATCH = 4
CHUNKS = 4
EARLY = 3
HALVES = 2
F32 = jnp.float32
BF16 = jnp.bfloat16
MESH = pl.DeviceIdType.MESH
Z_ORDER = (4, 3, 5, 2, 6, 1, 7)
NT = (((1,), (1,)), ((), ()))
PAIR, SELK, JSEL, RET, TAB = 0, 12, 24, 27, 43


def scan_pairs(pa_s, tab, z, y):
    def visit(p, carry):
        counts, found = carry
        counts, found = list(counts), list(found)
        for j in range(NY):
            atom = z * NY + ((y + j) & (NY - 1))
            hit = (pa_s[0, p] == atom) | (pa_s[1, p] == atom)
            for s in range(CAP):
                found[j * CAP + s] = jnp.where(hit & (counts[j] == s), p, found[j * CAP + s])
            counts[j] = counts[j] + hit.astype(jnp.int32)
        return tuple(counts), tuple(found)

    zero, none = jnp.int32(0), jnp.int32(-1)
    _, found = lax.fori_loop(0, NZ * NY, visit, ((zero,) * NY, (none,) * (NY * CAP)))
    for i in range(NY * CAP):
        pair = jnp.maximum(found[i], 0)
        tab[PAIR + i] = found[i]
        tab[SELK + i] = (z - (pair >> 2)) & (NZ - 1)
        if i < CAP:
            tab[JSEL + i] = (y - (pair & (NY - 1))) & (NY - 1)
    for k in range(NZ):
        pair = ((z + k) & (NZ - 1)) * NY + y
        for i in range(2):
            atom = pa_s[i, pair]
            j = (y - (atom & (NY - 1))) & (NY - 1)
            mate = ((NY - j) & (NY - 1)) * CAP
            rank = jnp.where(tab[PAIR + mate + 1] == pair, 1, 0) + jnp.where(
                tab[PAIR + mate + 2] == pair, 2, 0
            )
            tab[RET + 2 * k + i] = jnp.where((atom >> 2) == z, j * CAP + rank, -1)


def scratch(npno, npao, kaux):
    vm, dma, sm = pltpu.VMEM, pltpu.SemaphoreType.DMA, pltpu.SMEM
    rows = npno // CHUNKS
    square = (npno, npno)
    part = (npno // HALVES, npno)
    shapes = {
        "pa_s": sm((2, NZ * NY), jnp.int32),
        "pn_s": sm((1, NOV), jnp.int32),
        "sh_s": sm((1,), F32),
        "e_v": vm((1, npno), F32),
        "tab": sm((TAB,), jnp.int32),
        "f_v": vm((kaux, npao, npao), BF16),
        "s_v": vm((NOV,) + square, BF16),
        "i_v": vm(square, F32),
        "b_v": vm((npao, npno), BF16),
        "n_in": vm((NY - 1, 1, NOV), jnp.int32),
        "n_s": sm((NY - 1, 1, NOV), jnp.int32),
        "lhs_a": vm((CAP * EARLY * rows, npao), BF16),
        "lhs_b": vm((CAP * (CHUNKS - EARLY) * rows, npao), BF16),
        "b_t": vm((CAP, npno, npao), BF16),
        "half": vm((CAP, kaux * npno, npao), BF16),
        "g_v": vm((CAP, npno, kaux * npno), BF16),
        "p_v": vm((CAP, npno, kaux * npno), BF16),
        "cc": vm((CAP, 2 * npno, 2 * npno), BF16),
        "den": vm(square, F32),
        "base": vm(square, F32),
        "mine": vm(square, F32),
        "loc": dma((11,)),
        "nx": (dma((NY - 1,)), dma((NY - 1,))),
    }
    for c in range(CHUNKS):
        shapes[f"zb{c}"] = vm((NZ, rows, npao), BF16)
        shapes[f"ybo{c}"] = vm((NY - 1, CAP, rows, npao), BF16)
        shapes[f"yb{c}"] = vm((NY, CAP, rows, npao), BF16)
    shapes["zb"] = (dma((CHUNKS, NZ - 1)), dma((CHUNKS, NZ - 1)))
    shapes["yb"] = (dma((CHUNKS, NY - 1)), dma((CHUNKS, NY - 1)))
    for it in range(ITERS):
        for h in range(HALVES):
            shapes[f"zc{it}{h}"] = vm((NZ,) + part, BF16)
            shapes[f"nc{it}{h}"] = vm((2 * NZ,) + part, BF16)
            shapes[f"yt{it}{h}"] = vm((NY * CAP,) + part, BF16)
        for s in range(CAP):
            shapes[f"yc{it}{s}"] = vm((NY, HALVES) + part, BF16)
        shapes[f"yco{it}"] = vm((HALVES, CAP, NY - 1) + part, BF16)
        shapes[f"yn{it}"] = vm((NY, NOV) + square, BF16)
        shapes[f"yno{it}"] = vm((NY - 1, NOV) + square, BF16)
        shapes[f"bk{it}"] = vm((HALVES, NZ) + part, BF16)
        shapes[f"zt{it}"] = vm((HALVES, NZ) + part, BF16)
    shapes["zc"] = (dma((ITERS, HALVES, NZ - 1)), dma((ITERS, HALVES, NZ - 1)))
    shapes["yc"] = (dma((ITERS, HALVES, CAP, NY - 1)), dma((ITERS, HALVES, CAP, NY - 1)))
    shapes["fw"] = (dma((ITERS, HALVES)), dma((ITERS, HALVES)))
    shapes["yn"] = (dma((ITERS, NY - 1)), dma((ITERS, NY - 1)))
    shapes["yt"] = (dma((ITERS, HALVES, CAP, NY - 1)), dma((ITERS, HALVES, CAP, NY - 1)))
    shapes["zt"] = (dma((ITERS, HALVES, NZ - 1)), dma((ITERS, HALVES, NZ - 1)))
    flat = {}
    for name, shape in shapes.items():
        if isinstance(shape, tuple):
            flat[name + "_s"], flat[name + "_r"] = shape
        else:
            flat[name] = shape
    return flat


def kernel(names, pa_h, pn_h, sh_h, e_h, b_h, c_h, f_h, s_h, i_h, out, *refs):
    r = dict(zip(names, refs))
    tab, loc, half, g_v, p_v, cc = r["tab"], r["loc"], r["half"], r["g_v"], r["p_v"], r["cc"]
    g = lax.axis_index("grp")
    d = lax.axis_index("dev")
    z, y = d // NY, d % NY
    groups = lax.axis_size("grp")
    npno = c_h.shape[1]
    kaux = f_h.shape[0]
    rows = npno // CHUNKS
    part = npno // HALVES
    span_of = [pl.ds(h * part, part) for h in range(HALVES)]

    def at_z(k):
        return {"grp": g, "dev": ((z + k) % NZ) * NY + y}

    def at_y(j):
        return {"grp": g, "dev": z * NY + (y + j) % NY}

    before = {"grp": (g + groups - 1) % groups, "dev": d}
    after = {"grp": (g + 1) % groups, "dev": d}

    sent = []

    def send(src, dst, name, index, where):
        copy = pltpu.make_async_remote_copy(
            src_ref=src, dst_ref=dst,
            send_sem=r[name + "_s"].at[index], recv_sem=r[name + "_r"].at[index],
            device_id=where, device_id_type=MESH,
        )
        copy.start()
        sent.append(copy)
        return copy

    def arrive(copies):
        for copy in copies:
            copy.wait_recv()

    def local(src, dst, number):
        copy = pltpu.make_async_copy(src, dst, loc.at[number])
        copy.start()
        return copy

    own_b = local(b_h, r["b_v"], 0)
    small = [
        local(pa_h, r["pa_s"], 1),
        local(pn_h, r["pn_s"], 2),
        local(sh_h, r["sh_s"], 3),
        local(e_h, r["e_v"], 4),
    ]
    own_c = [local(c_h.at[span_of[h]], r[f"zc0{h}"].at[0], (5, 10)[h]) for h in range(HALVES)]
    own_f = local(f_h, r["f_v"], 6)
    own_s = local(s_h, r["s_v"], 7)
    own_i = local(i_h, r["i_v"], 8)

    barrier = pltpu.get_barrier_semaphore()
    partners = [at_z(k) for k in Z_ORDER] + [at_y(j) for j in range(1, NY)] + [before, after]
    for partner in partners:
        pl.semaphore_signal(barrier, inc=1, device_id=partner, device_id_type=MESH)
    cc[...] = jnp.zeros_like(cc)
    own_b.wait()
    flipped = r["b_v"][...].T
    for c in range(CHUNKS):
        r[f"zb{c}"][0] = flipped[c * rows:(c + 1) * rows]
    for copy in small:
        copy.wait()
    scan_pairs(r["pa_s"], tab, z, y)
    wide = jnp.broadcast_to(r["e_v"][...], (npno, npno))
    r["den"][...] = wide + wide.T + r["sh_s"][0]
    for copy in own_c:
        copy.wait()
    pl.semaphore_wait(barrier, len(partners))

    zb = [
        [send(r[f"zb{c}"].at[0], r[f"zb{c}"].at[k], "zb", (c, k - 1), at_z(k)) for k in Z_ORDER]
        for c in range(CHUNKS)
    ]
    zc = [
        [
            send(c_h.at[span_of[h]], r[f"zc0{h}"].at[k], "zc", (0, h, k - 1), at_z(k))
            for k in Z_ORDER
        ]
        for h in range(HALVES)
    ]
    nx = [send(pn_h, r["n_in"].at[j - 1], "nx", j - 1, at_y(j)) for j in range(1, NY)]

    yb = []
    for c in range(CHUNKS):
        arrive(zb[c])
        for j in range(1, NY):
            for s in range(CAP):
                r[f"ybo{c}"][j - 1, s] = r[f"zb{c}"][tab[SELK + j * CAP + s]]
            yb.append(
                send(r[f"ybo{c}"].at[j - 1], r[f"yb{c}"].at[j], "yb", (c, j - 1), at_y(j))
            )
        for s in range(CAP):
            r[f"yb{c}"][0, s] = r[f"zb{c}"][tab[SELK + s]]

    def collect(first, last, lhs):
        height = (last - first) * rows
        for s in range(CAP):
            for c in range(first, last):
                block = r[f"yb{c}"][tab[JSEL + s], s]
                lhs[pl.ds(s * height + (c - first) * rows, rows), :] = block
                r["b_t"][s, pl.ds(c * rows, rows), :] = block

    def first_product(first, last, lhs):
        height = (last - first) * rows

        def step(kk, carry):
            for u in range(BATCH):
                part = jnp.dot(
                    lhs[...], r["f_v"][kk * BATCH + u], preferred_element_type=F32
                ).astype(BF16)
                start = pl.multiple_of(kk * (npno * BATCH), npno * BATCH)
                for s in range(CAP):
                    half[s, pl.ds(start + u * npno + first * rows, height), :] = part[
                        s * height:(s + 1) * height
                    ]
            return carry

        lax.fori_loop(0, kaux // BATCH, step, 0)

    def share_amps(it, zc):
        yc, fw = [[] for s in range(CAP)], []
        for h in range(HALVES):
            column, beside = r[f"zc{it}{h}"], r[f"nc{it}{h}"]
            arrive(zc[h])
            for s in range(CAP):
                for j in range(1, NY):
                    r[f"yco{it}"][h, s, j - 1] = column[tab[SELK + j * CAP + s]]
                yc[s] += [
                    send(
                        r[f"yco{it}"].at[h, s, j - 1], r[f"yc{it}{s}"].at[j, h],
                        "yc", (it, h, s, j - 1), at_y(j),
                    )
                    for j in range(1, NY)
                ]
                r[f"yc{it}{s}"][0, h] = column[tab[SELK + s]]
            fw.append(send(column, beside.at[pl.ds(NZ, NZ)], "fw", (it, h), before))
            beside[:NZ] = column[...]
        return yc, fw

    def place(listed):
        return (listed >> 5) * NZ + ((z - ((listed & 31) >> 2)) & (NZ - 1))

    def share_neighbours(it, fw):
        arrive(fw)
        yn = []
        for j in range(1, NY):
            for n in range(NOV):
                index = place(r["n_s"][NY - 1 - j, 0, n])
                for h in range(HALVES):
                    r[f"yno{it}"][j - 1, n, span_of[h], :] = r[f"nc{it}{h}"][index]
            yn.append(
                send(r[f"yno{it}"].at[j - 1], r[f"yn{it}"].at[j], "yn", (it, j - 1), at_y(j))
            )
        for n in range(NOV):
            index = place(r["pn_s"][0, n])
            for h in range(HALVES):
                r[f"yn{it}"][0, n, span_of[h], :] = r[f"nc{it}{h}"][index]
        return yn

    arrive(nx)
    to_s = local(r["n_in"], r["n_s"], 9)
    own_f.wait()
    arrive(yb[:EARLY * (NY - 1)])
    collect(0, EARLY, r["lhs_a"])
    first_product(0, EARLY, r["lhs_a"])
    yc, fw = share_amps(0, zc)
    arrive(yb[EARLY * (NY - 1):])
    collect(EARLY, CHUNKS, r["lhs_b"])
    first_product(EARLY, CHUNKS, r["lhs_b"])

    def second_product(kk, carry):
        start = pl.multiple_of(kk * (npno * BATCH), npno * BATCH)
        for s in range(CAP):
            inner = lax.dot_general(
                half[s, pl.ds(start, npno * BATCH), :], r["b_t"][s], NT,
                preferred_element_type=F32,
            ).astype(BF16)
            for u in range(BATCH):
                g_v[s, :, pl.ds(start + u * npno, npno)] = inner[u * npno:(u + 1) * npno]
        return carry

    lax.fori_loop(0, kaux // BATCH, second_product, 0)
    to_s.wait()
    own_s.wait()
    own_i.wait()

    for it in range(ITERS):
        yt = [[] for h in range(HALVES)]

        def send_term(s, h):
            home = r[f"yt{it}{h}"]
            for j in range(1, NY):
                yt[h].append(
                    send(home.at[s], home.at[j * CAP + s], "yt", (it, h, s, j - 1), at_y(j))
                )

        for s in range(CAP):
            arrive(yc[s])
            amps = r[f"yc{it}{s}"][tab[JSEL + s]]
            for h in range(HALVES):
                cc[s, h * part:(h + 1) * part, :npno] = amps[h]
                cc[s, npno + h * part:npno + (h + 1) * part, npno:] = amps[h]
            for b in range(kaux // 2):
                span = pl.ds(b * 2 * npno, 2 * npno)
                p_v[s, :, span] = jnp.dot(
                    g_v[s, :, span], cc[s], preferred_element_type=F32
                ).astype(BF16)
            term = lax.dot_general(p_v[s], g_v[s], NT, preferred_element_type=F32).astype(BF16)
            for h in range(HALVES):
                r[f"yt{it}{h}"][s] = term[h * part:(h + 1) * part]
            send_term(s, 0)
            if s == 0:
                send_term(s, 1)
        for s in range(1, CAP):
            send_term(s, 1)
        yn = share_neighbours(it, fw)
        zt = []
        for h in range(HALVES):
            arrive(yt[h])
            copies = []
            for k in Z_ORDER + (0,):
                total = jnp.zeros((part, npno), F32)
                for i in range(2):
                    slot = tab[RET + 2 * k + i]
                    weight = (slot >= 0).astype(F32)
                    total += r[f"yt{it}{h}"][jnp.maximum(slot, 0)].astype(F32) * weight
                if k == 0:
                    r["mine"][span_of[h], :] = total
                else:
                    r[f"bk{it}"][h, k] = total.astype(BF16)
                    copies.append(
                        send(
                            r[f"bk{it}"].at[h, k], r[f"zt{it}"].at[h, k],
                            "zt", (it, h, k - 1), at_z(k),
                        )
                    )
            zt.append(copies)
        arrive(yn)
        coupling = r["i_v"][...]
        for n in range(NOV):
            other = r[f"yn{it}"][(y - (r["pn_s"][0, n] & (NY - 1))) & (NY - 1), n]
            mixed = jnp.dot(r["s_v"][n], other, preferred_element_type=F32).astype(BF16)
            coupling += lax.dot_general(mixed, r["s_v"][n], NT, preferred_element_type=F32)
        r["base"][...] = coupling
        zc = []
        for h in range(HALVES):
            arrive(zt[h])
            total = r["base"][span_of[h], :] + r["mine"][span_of[h], :]
            for k in range(1, NZ):
                total += r[f"zt{it}"][h, k].astype(F32)
            if it + 1 < ITERS:
                column = r[f"zc{it + 1}{h}"]
                column[0] = (-total / r["den"][span_of[h], :]).astype(BF16)
                zc.append([
                    send(column.at[0], column.at[k], "zc", (it + 1, h, k - 1), at_z(k))
                    for k in Z_ORDER
                ])
            else:
                out[span_of[h], :] = total
        if it + 1 < ITERS:
            yc, fw = share_amps(it + 1, zc)
    for copy in sent:
        copy.wait_send()


def on_device(
    amplitudes,
    bases,
    factors,
    intersections,
    pair_integrals,
    pno_energies,
    pair_shift,
    pair_atoms,
    pair_next,
):
    npno, npao, kaux = amplitudes.shape[1], bases.shape[1], factors.shape[1]
    shapes = scratch(npno, npao, kaux)
    names = tuple(shapes)

    def body(*refs):
        kernel(names, *refs)

    total = pl.pallas_call(
        body,
        out_shape=jax.ShapeDtypeStruct((npno, npno), F32),
        in_specs=[pl.BlockSpec(memory_space=pl.ANY)] * 9,
        out_specs=pl.BlockSpec(memory_space=pltpu.VMEM),
        scratch_shapes=list(shapes.values()),
        compiler_params=pltpu.CompilerParams(
            collective_id=0, has_side_effects=True, vmem_limit_bytes=67043328
        ),
        name="ladder",
    )(
        pair_atoms.T, pair_next, pair_shift, pno_energies, bases[0], amplitudes[0], factors[0],
        intersections[0], pair_integrals[0],
    )
    denominator = pno_energies[0][:, None] + pno_energies[0][None, :] + pair_shift[0]
    return (-total / denominator)[None]


def solution(mesh):
    return jax.shard_map(
        on_device,
        mesh=mesh,
        in_specs=(
            P(("grp", "dev"), None, None),
            P(("grp", "dev"), None, None),
            P(("grp", "dev"), None, None, None),
            P(("grp", "dev"), None, None, None),
            P(("grp", "dev"), None, None),
            P(("grp", "dev"), None),
            P(("grp", "dev")),
            P("grp", None),
            P(("grp", "dev"), None),
        ),
        out_specs=P(("grp", "dev"), None, None),
        check_vma=False,
    )
```

```python
import jax
import jax.numpy as jnp
from jax import lax
from jax.experimental import pallas as pl
from jax.experimental.pallas import tpu as pltpu
from jax.sharding import PartitionSpec as P

CAP = 3
ITERS = 2
NZ = 8
NY = 4
NOV = 4
BATCH = 8
CHUNKS = 4
EARLY = 3
HALVES = 2
F32 = jnp.float32
BF16 = jnp.bfloat16
MESH = pl.DeviceIdType.MESH
Z_ORDER = (4, 3, 5, 2, 6, 1, 7)
NT = (((1,), (1,)), ((), ()))
PAIR, SELK, JSEL, RET, TAB = 0, 12, 24, 27, 43


def scan_pairs(pa_s, tab, z, y):
    def visit(p, carry):
        counts, found = carry
        counts, found = list(counts), list(found)
        for j in range(NY):
            atom = z * NY + ((y + j) & (NY - 1))
            hit = (pa_s[0, p] == atom) | (pa_s[1, p] == atom)
            for s in range(CAP):
                found[j * CAP + s] = jnp.where(hit & (counts[j] == s), p, found[j * CAP + s])
            counts[j] = counts[j] + hit.astype(jnp.int32)
        return tuple(counts), tuple(found)

    zero, none = jnp.int32(0), jnp.int32(-1)
    _, found = lax.fori_loop(0, NZ * NY, visit, ((zero,) * NY, (none,) * (NY * CAP)))
    for i in range(NY * CAP):
        pair = jnp.maximum(found[i], 0)
        tab[PAIR + i] = found[i]
        tab[SELK + i] = (z - (pair >> 2)) & (NZ - 1)
        if i < CAP:
            tab[JSEL + i] = (y - (pair & (NY - 1))) & (NY - 1)
    for k in range(NZ):
        pair = ((z + k) & (NZ - 1)) * NY + y
        for i in range(2):
            atom = pa_s[i, pair]
            j = (y - (atom & (NY - 1))) & (NY - 1)
            mate = ((NY - j) & (NY - 1)) * CAP
            rank = jnp.where(tab[PAIR + mate + 1] == pair, 1, 0) + jnp.where(
                tab[PAIR + mate + 2] == pair, 2, 0
            )
            tab[RET + 2 * k + i] = jnp.where((atom >> 2) == z, j * CAP + rank, -1)


def scratch(npno, npao, kaux):
    vm, dma, sm = pltpu.VMEM, pltpu.SemaphoreType.DMA, pltpu.SMEM
    rows = npno // CHUNKS
    square = (npno, npno)
    part = (npno // HALVES, npno)
    shapes = {
        "pa_s": sm((2, NZ * NY), jnp.int32),
        "pn_s": sm((1, NOV), jnp.int32),
        "sh_s": sm((1,), F32),
        "e_v": vm((1, npno), F32),
        "tab": sm((TAB,), jnp.int32),
        "f_v": vm((kaux, npao, npao), BF16),
        "s_v": vm((NOV,) + square, BF16),
        "i_v": vm(square, F32),
        "b_v": vm((npao, npno), BF16),
        "n_in": vm((NY - 1, 1, NOV), jnp.int32),
        "n_s": sm((NY - 1, 1, NOV), jnp.int32),
        "lhs_a": vm((CAP * EARLY * rows, npao), BF16),
        "lhs_b": vm((CAP * (CHUNKS - EARLY) * rows, npao), BF16),
        "b_t": vm((CAP, npno, npao), BF16),
        "half": vm((CAP, kaux * npno, npao), BF16),
        "g_v": vm((CAP, npno, kaux * npno), BF16),
        "p_v": vm((CAP, npno, kaux * npno), BF16),
        "cc": vm((CAP, 2 * npno, 2 * npno), BF16),
        "den": vm(square, F32),
        "base": vm(square, F32),
        "mine": vm(square, F32),
        "loc": dma((13,)),
        "nx": (dma((NY - 1,)), dma((NY - 1,))),
    }
    for c in range(CHUNKS):
        shapes[f"zb{c}"] = vm((NZ, rows, npao), BF16)
        shapes[f"ybo{c}"] = vm((NY - 1, CAP, rows, npao), BF16)
        shapes[f"yb{c}"] = vm((NY, CAP, rows, npao), BF16)
    shapes["zb"] = (dma((CHUNKS, NZ - 1)), dma((CHUNKS, NZ - 1)))
    shapes["yb"] = (dma((CHUNKS, NY - 1)), dma((CHUNKS, NY - 1)))
    for it in range(ITERS):
        for h in range(HALVES):
            shapes[f"zc{it}{h}"] = vm((NZ,) + part, BF16)
            shapes[f"nc{it}{h}"] = vm((2 * NZ,) + part, BF16)
            shapes[f"yt{it}{h}"] = vm((NY * CAP,) + part, BF16)
        for s in range(CAP):
            shapes[f"yc{it}{s}"] = vm((NY, HALVES) + part, BF16)
        shapes[f"yco{it}"] = vm((HALVES, CAP, NY - 1) + part, BF16)
        shapes[f"yn{it}"] = vm((NY, NOV) + square, BF16)
        shapes[f"yno{it}"] = vm((NY - 1, NOV) + square, BF16)
        shapes[f"bk{it}"] = vm((HALVES, NZ) + part, BF16)
        shapes[f"zt{it}"] = vm((HALVES, NZ) + part, BF16)
    shapes["zc"] = (dma((ITERS, HALVES, NZ - 1)), dma((ITERS, HALVES, NZ - 1)))
    shapes["yc"] = (dma((ITERS, HALVES, CAP, NY - 1)), dma((ITERS, HALVES, CAP, NY - 1)))
    shapes["fw"] = (dma((ITERS, HALVES)), dma((ITERS, HALVES)))
    shapes["yn"] = (dma((ITERS, NY - 1)), dma((ITERS, NY - 1)))
    shapes["yt"] = (dma((ITERS, HALVES, CAP, NY - 1)), dma((ITERS, HALVES, CAP, NY - 1)))
    shapes["zt"] = (dma((ITERS, HALVES, NZ - 1)), dma((ITERS, HALVES, NZ - 1)))
    flat = {}
    for name, shape in shapes.items():
        if isinstance(shape, tuple):
            flat[name + "_s"], flat[name + "_r"] = shape
        else:
            flat[name] = shape
    return flat


def kernel(names, pa_h, pn_h, sh_h, e_h, b_h, c_h, f_h, s_h, i_h, out, *refs):
    r = dict(zip(names, refs))
    tab, loc, half, g_v, p_v, cc = r["tab"], r["loc"], r["half"], r["g_v"], r["p_v"], r["cc"]
    g = lax.axis_index("grp")
    d = lax.axis_index("dev")
    z, y = d // NY, d % NY
    groups = lax.axis_size("grp")
    npno = c_h.shape[1]
    kaux = f_h.shape[0]
    rows = npno // CHUNKS
    part = npno // HALVES
    span_of = [pl.ds(h * part, part) for h in range(HALVES)]

    def at_z(k):
        return {"grp": g, "dev": ((z + k) % NZ) * NY + y}

    def at_y(j):
        return {"grp": g, "dev": z * NY + (y + j) % NY}

    before = {"grp": (g + groups - 1) % groups, "dev": d}
    after = {"grp": (g + 1) % groups, "dev": d}

    sent = []

    def send(src, dst, name, index, where):
        copy = pltpu.make_async_remote_copy(
            src_ref=src, dst_ref=dst,
            send_sem=r[name + "_s"].at[index], recv_sem=r[name + "_r"].at[index],
            device_id=where, device_id_type=MESH,
        )
        copy.start()
        sent.append(copy)
        return copy

    def arrive(copies):
        for copy in copies:
            copy.wait_recv()

    def local(src, dst, number):
        copy = pltpu.make_async_copy(src, dst, loc.at[number])
        copy.start()
        return copy

    own_b = local(b_h, r["b_v"], 0)
    small = [
        local(pa_h, r["pa_s"], 1),
        local(pn_h, r["pn_s"], 2),
        local(sh_h, r["sh_s"], 3),
        local(e_h, r["e_v"], 4),
    ]
    own_c = [local(c_h.at[span_of[h]], r[f"zc0{h}"].at[0], (5, 10, 11, 12)[h]) for h in range(HALVES)]
    own_f = local(f_h, r["f_v"], 6)
    own_s = local(s_h, r["s_v"], 7)
    own_i = local(i_h, r["i_v"], 8)

    barrier = pltpu.get_barrier_semaphore()
    partners = [at_z(k) for k in Z_ORDER] + [at_y(j) for j in range(1, NY)] + [before, after]
    for partner in partners:
        pl.semaphore_signal(barrier, inc=1, device_id=partner, device_id_type=MESH)
    cc[...] = jnp.zeros_like(cc)
    own_b.wait()
    flipped = r["b_v"][...].T
    for c in range(CHUNKS):
        r[f"zb{c}"][0] = flipped[c * rows:(c + 1) * rows]
    for copy in small:
        copy.wait()
    scan_pairs(r["pa_s"], tab, z, y)
    wide = jnp.broadcast_to(r["e_v"][...], (npno, npno))
    r["den"][...] = wide + wide.T + r["sh_s"][0]
    for copy in own_c:
        copy.wait()
    pl.semaphore_wait(barrier, len(partners))

    zb = [{} for c in range(CHUNKS)]

    def direct(c):
        for k in (2, 6, 1, 7):
            zb[c][k] = send(r[f"zb{c}"].at[0], r[f"zb{c}"].at[k], "zb", (c, k - 1), at_z(k))

    def relay(c):
        block = r[f"zb{c}"]
        for held, hop, ahead in ((2, 1, 3), (6, 7, 5)):
            zb[c][held].wait_recv()
            if (held == 2) == (c % 2 == 0):
                zb[c][4] = send(block.at[held], block.at[4], "zb", (c, 3), at_z(held))
            zb[c][ahead] = send(block.at[held], block.at[ahead], "zb", (c, ahead - 1), at_z(hop))

    yb = []

    def cross(c):
        arrive([zb[c][k] for k in (1, 7, 3, 5, 4)])
        for j in range(1, NY):
            for s in range(CAP):
                r[f"ybo{c}"][j - 1, s] = r[f"zb{c}"][tab[SELK + j * CAP + s]]
            yb.append(
                send(r[f"ybo{c}"].at[j - 1], r[f"yb{c}"].at[j], "yb", (c, j - 1), at_y(j))
            )
        for s in range(CAP):
            r[f"yb{c}"][0, s] = r[f"zb{c}"][tab[SELK + s]]

    for c in range(CHUNKS - 1):
        direct(c)
    relay(0)
    direct(CHUNKS - 1)
    for c in range(1, CHUNKS - 1):
        relay(c)
    cross(0)
    relay(CHUNKS - 1)
    zc = [
        [
            send(c_h.at[span_of[h]], r[f"zc0{h}"].at[k], "zc", (0, h, k - 1), at_z(k))
            for k in Z_ORDER
        ]
        for h in range(HALVES)
    ]
    nx = [send(pn_h, r["n_in"].at[j - 1], "nx", j - 1, at_y(j)) for j in range(1, NY)]
    for c in range(1, CHUNKS):
        cross(c)

    def collect(first, last, lhs):
        height = (last - first) * rows
        for s in range(CAP):
            for c in range(first, last):
                block = r[f"yb{c}"][tab[JSEL + s], s]
                lhs[pl.ds(s * height + (c - first) * rows, rows), :] = block
                r["b_t"][s, pl.ds(c * rows, rows), :] = block

    def first_product(first, last, lhs):
        height = (last - first) * rows

        def step(kk, carry):
            for u in range(BATCH):
                part = jnp.dot(
                    lhs[...], r["f_v"][kk * BATCH + u], preferred_element_type=F32
                ).astype(BF16)
                start = pl.multiple_of(kk * (npno * BATCH), npno * BATCH)
                for s in range(CAP):
                    half[s, pl.ds(start + u * npno + first * rows, height), :] = part[
                        s * height:(s + 1) * height
                    ]
            return carry

        lax.fori_loop(0, kaux // BATCH, step, 0)

    def share_half(it, h, copies, yc, fw):
        column, beside = r[f"zc{it}{h}"], r[f"nc{it}{h}"]
        arrive(copies)
        for s in range(CAP):
            for j in range(1, NY):
                r[f"yco{it}"][h, s, j - 1] = column[tab[SELK + j * CAP + s]]
            yc[s] += [
                send(
                    r[f"yco{it}"].at[h, s, j - 1], r[f"yc{it}{s}"].at[j, h],
                    "yc", (it, h, s, j - 1), at_y(j),
                )
                for j in range(1, NY)
            ]
            r[f"yc{it}{s}"][0, h] = column[tab[SELK + s]]
        fw.append(send(column, beside.at[pl.ds(NZ, NZ)], "fw", (it, h), before))
        beside[:NZ] = column[...]

    def place(listed):
        return (listed >> 5) * NZ + ((z - ((listed & 31) >> 2)) & (NZ - 1))

    def share_neighbours(it, fw):
        arrive(fw)
        yn = []
        for j in range(1, NY):
            for n in range(NOV):
                index = place(r["n_s"][NY - 1 - j, 0, n])
                for h in range(HALVES):
                    r[f"yno{it}"][j - 1, n, span_of[h], :] = r[f"nc{it}{h}"][index]
            yn.append(
                send(r[f"yno{it}"].at[j - 1], r[f"yn{it}"].at[j], "yn", (it, j - 1), at_y(j))
            )
        for n in range(NOV):
            index = place(r["pn_s"][0, n])
            for h in range(HALVES):
                r[f"yn{it}"][0, n, span_of[h], :] = r[f"nc{it}{h}"][index]
        return yn

    arrive(nx)
    to_s = local(r["n_in"], r["n_s"], 9)
    own_f.wait()
    arrive(yb[:EARLY * (NY - 1)])
    collect(0, EARLY, r["lhs_a"])
    yc, fw = [[] for s in range(CAP)], []
    first_product(0, EARLY, r["lhs_a"])
    share_half(0, 0, zc[0], yc, fw)
    share_half(0, 1, zc[1], yc, fw)
    arrive(yb[EARLY * (NY - 1):])
    collect(EARLY, CHUNKS, r["lhs_b"])
    first_product(EARLY, CHUNKS, r["lhs_b"])

    def second_product(kk, carry):
        start = pl.multiple_of(kk * (npno * BATCH), npno * BATCH)
        for s in range(CAP):
            inner = lax.dot_general(
                half[s, pl.ds(start, npno * BATCH), :], r["b_t"][s], NT,
                preferred_element_type=F32,
            ).astype(BF16)
            for u in range(BATCH):
                g_v[s, :, pl.ds(start + u * npno, npno)] = inner[u * npno:(u + 1) * npno]
        return carry

    lax.fori_loop(0, kaux // BATCH, second_product, 0)
    to_s.wait()
    own_s.wait()
    own_i.wait()

    for it in range(ITERS):
        yt = [[] for h in range(HALVES)]

        def send_term(s, h):
            home = r[f"yt{it}{h}"]
            for j in range(1, NY):
                yt[h].append(
                    send(home.at[s], home.at[j * CAP + s], "yt", (it, h, s, j - 1), at_y(j))
                )

        for s in range(CAP):
            arrive(yc[s])
            amps = r[f"yc{it}{s}"][tab[JSEL + s]]
            for h in range(HALVES):
                cc[s, h * part:(h + 1) * part, :npno] = amps[h]
                cc[s, npno + h * part:npno + (h + 1) * part, npno:] = amps[h]
            for b in range(kaux // 2):
                span = pl.ds(b * 2 * npno, 2 * npno)
                p_v[s, :, span] = jnp.dot(
                    g_v[s, :, span], cc[s], preferred_element_type=F32
                ).astype(BF16)
            term = lax.dot_general(p_v[s], g_v[s], NT, preferred_element_type=F32).astype(BF16)
            for h in range(HALVES):
                r[f"yt{it}{h}"][s] = term[h * part:(h + 1) * part]
            for h in range(HALVES if s == 0 else 1):
                send_term(s, h)
        for h in range(1, HALVES):
            for s in range(1, CAP):
                send_term(s, h)
        yn = share_neighbours(it, fw)
        zt = []
        for h in range(HALVES):
            arrive(yt[h])
            copies = []
            for k in Z_ORDER + (0,):
                total = jnp.zeros((part, npno), F32)
                for i in range(2):
                    slot = tab[RET + 2 * k + i]
                    weight = (slot >= 0).astype(F32)
                    total += r[f"yt{it}{h}"][jnp.maximum(slot, 0)].astype(F32) * weight
                if k == 0:
                    r["mine"][span_of[h], :] = total
                else:
                    r[f"bk{it}"][h, k] = total.astype(BF16)
                    copies.append(
                        send(
                            r[f"bk{it}"].at[h, k], r[f"zt{it}"].at[h, k],
                            "zt", (it, h, k - 1), at_z(k),
                        )
                    )
            zt.append(copies)
        arrive(yn)
        coupling = r["i_v"][...]
        for n in range(NOV):
            other = r[f"yn{it}"][(y - (r["pn_s"][0, n] & (NY - 1))) & (NY - 1), n]
            mixed = jnp.dot(r["s_v"][n], other, preferred_element_type=F32).astype(BF16)
            coupling += lax.dot_general(mixed, r["s_v"][n], NT, preferred_element_type=F32)
        r["base"][...] = coupling
        zc = []
        for h in range(HALVES):
            arrive(zt[h])
            total = r["base"][span_of[h], :] + r["mine"][span_of[h], :]
            for k in range(1, NZ):
                total += r[f"zt{it}"][h, k].astype(F32)
            if it + 1 < ITERS:
                column = r[f"zc{it + 1}{h}"]
                column[0] = (-total / r["den"][span_of[h], :]).astype(BF16)
                zc.append([
                    send(column.at[0], column.at[k], "zc", (it + 1, h, k - 1), at_z(k))
                    for k in Z_ORDER
                ])
            else:
                out[span_of[h], :] = total
        if it + 1 < ITERS:
            yc, fw = [[] for s in range(CAP)], []
            for h in range(HALVES):
                share_half(it + 1, h, zc[h], yc, fw)
    for copy in sent:
        copy.wait_send()


def on_device(
    amplitudes,
    bases,
    factors,
    intersections,
    pair_integrals,
    pno_energies,
    pair_shift,
    pair_atoms,
    pair_next,
):
    npno, npao, kaux = amplitudes.shape[1], bases.shape[1], factors.shape[1]
    shapes = scratch(npno, npao, kaux)
    names = tuple(shapes)

    def body(*refs):
        kernel(names, *refs)

    total = pl.pallas_call(
        body,
        out_shape=jax.ShapeDtypeStruct((npno, npno), F32),
        in_specs=[pl.BlockSpec(memory_space=pl.ANY)] * 9,
        out_specs=pl.BlockSpec(memory_space=pltpu.VMEM),
        scratch_shapes=list(shapes.values()),
        compiler_params=pltpu.CompilerParams(
            collective_id=0, has_side_effects=True, vmem_limit_bytes=67043328
        ),
        name="ladder",
    )(
        pair_atoms.T, pair_next, pair_shift, pno_energies, bases[0], amplitudes[0], factors[0],
        intersections[0], pair_integrals[0],
    )
    denominator = pno_energies[0][:, None] + pno_energies[0][None, :] + pair_shift[0]
    return (-total / denominator)[None]


def solution(mesh):
    return jax.shard_map(
        on_device,
        mesh=mesh,
        in_specs=(
            P(("grp", "dev"), None, None),
            P(("grp", "dev"), None, None),
            P(("grp", "dev"), None, None, None),
            P(("grp", "dev"), None, None, None),
            P(("grp", "dev"), None, None),
            P(("grp", "dev"), None),
            P(("grp", "dev")),
            P("grp", None),
            P(("grp", "dev"), None),
        ),
        out_specs=P(("grp", "dev"), None, None),
        check_vma=False,
    )
```

```python
import jax
import jax.numpy as jnp
from jax import lax
from jax.experimental import pallas as pl
from jax.experimental.pallas import tpu as pltpu
from jax.sharding import PartitionSpec as P

CAP = 3
ITERS = 2
NZ = 8
NY = 4
NOV = 4
BATCH = 8
CHUNKS = 4
EARLY = 3
HALVES = 2
F32 = jnp.float32
BF16 = jnp.bfloat16
MESH = pl.DeviceIdType.MESH
Z_ORDER = (4, 3, 5, 2, 6, 1, 7)
Y_ORDER = (1, 3, 2)
NT = (((1,), (1,)), ((), ()))
PAIR, SELK, JSEL, RET, TAB = 0, 12, 24, 27, 43


def scan_pairs(pa_s, tab, z, y):
    def visit(p, carry):
        counts, found = carry
        counts, found = list(counts), list(found)
        for j in range(NY):
            atom = z * NY + ((y + j) & (NY - 1))
            hit = (pa_s[0, p] == atom) | (pa_s[1, p] == atom)
            for s in range(CAP):
                found[j * CAP + s] = jnp.where(hit & (counts[j] == s), p, found[j * CAP + s])
            counts[j] = counts[j] + hit.astype(jnp.int32)
        return tuple(counts), tuple(found)

    zero, none = jnp.int32(0), jnp.int32(-1)
    _, found = lax.fori_loop(0, NZ * NY, visit, ((zero,) * NY, (none,) * (NY * CAP)))
    for i in range(NY * CAP):
        pair = jnp.maximum(found[i], 0)
        tab[PAIR + i] = found[i]
        tab[SELK + i] = (z - (pair >> 2)) & (NZ - 1)
        if i < CAP:
            tab[JSEL + i] = (y - (pair & (NY - 1))) & (NY - 1)
    for k in range(NZ):
        pair = ((z + k) & (NZ - 1)) * NY + y
        for i in range(2):
            atom = pa_s[i, pair]
            j = (y - (atom & (NY - 1))) & (NY - 1)
            mate = ((NY - j) & (NY - 1)) * CAP
            rank = jnp.where(tab[PAIR + mate + 1] == pair, 1, 0) + jnp.where(
                tab[PAIR + mate + 2] == pair, 2, 0
            )
            tab[RET + 2 * k + i] = jnp.where((atom >> 2) == z, j * CAP + rank, -1)


def scratch(npno, npao, kaux):
    vm, dma, sm = pltpu.VMEM, pltpu.SemaphoreType.DMA, pltpu.SMEM
    rows = npno // CHUNKS
    square = (npno, npno)
    part = (npno // HALVES, npno)
    shapes = {
        "pa_s": sm((2, NZ * NY), jnp.int32),
        "pn_s": sm((1, NOV), jnp.int32),
        "sh_s": sm((1,), F32),
        "e_v": vm((1, npno), F32),
        "tab": sm((TAB,), jnp.int32),
        "f_v": vm((kaux, npao, npao), BF16),
        "s_v": vm((NOV,) + square, BF16),
        "i_v": vm(square, F32),
        "b_v": vm((npao, npno), BF16),
        "n_in": vm((NY - 1, 1, NOV), jnp.int32),
        "n_s": sm((NY - 1, 1, NOV), jnp.int32),
        "lhs_a": vm((CAP * EARLY * rows, npao), BF16),
        "lhs_b": vm((CAP * (CHUNKS - EARLY) * rows, npao), BF16),
        "b_t": vm((CAP, npno, npao), BF16),
        "half": vm((CAP, kaux * npno, npao), BF16),
        "g_v": vm((CAP, npno, kaux * npno), BF16),
        "p_v": vm((CAP, npno, kaux * npno), BF16),
        "cc": vm((CAP, 2 * npno, 2 * npno), BF16),
        "den": vm(square, F32),
        "base": vm(square, F32),
        "mine": vm(square, F32),
        "loc": dma((13,)),
        "nx": (dma((NY - 1,)), dma((NY - 1,))),
    }
    for c in range(CHUNKS):
        shapes[f"zb{c}"] = vm((NZ, rows, npao), BF16)
        shapes[f"ybo{c}"] = vm((NY - 1, CAP, rows, npao), BF16)
        shapes[f"yb{c}"] = vm((NY, CAP, rows, npao), BF16)
    shapes["zb"] = (dma((CHUNKS, NZ - 1)), dma((CHUNKS, NZ - 1)))
    shapes["yb"] = (dma((CHUNKS, NY - 1)), dma((CHUNKS, NY - 1)))
    for it in range(ITERS):
        for h in range(HALVES):
            shapes[f"zc{it}{h}"] = vm((NZ,) + part, BF16)
            shapes[f"nc{it}{h}"] = vm((2 * NZ,) + part, BF16)
            shapes[f"yt{it}{h}"] = vm((NY * CAP,) + part, BF16)
        for s in range(CAP):
            shapes[f"yc{it}{s}"] = vm((NY, HALVES) + part, BF16)
        shapes[f"yco{it}"] = vm((HALVES, CAP, NY - 1) + part, BF16)
        shapes[f"yn{it}"] = vm((NY, NOV) + square, BF16)
        shapes[f"yno{it}"] = vm((NY - 1, NOV) + square, BF16)
        shapes[f"bk{it}"] = vm((HALVES, NZ) + part, BF16)
        shapes[f"zt{it}"] = vm((HALVES, NZ) + part, BF16)
    shapes["zc"] = (dma((ITERS, HALVES, NZ - 1)), dma((ITERS, HALVES, NZ - 1)))
    shapes["yc"] = (dma((ITERS, HALVES, CAP, NY - 1)), dma((ITERS, HALVES, CAP, NY - 1)))
    shapes["fw"] = (dma((ITERS, HALVES)), dma((ITERS, HALVES)))
    shapes["yn"] = (dma((ITERS, NY - 1)), dma((ITERS, NY - 1)))
    shapes["yt"] = (dma((ITERS, HALVES, CAP, NY - 1)), dma((ITERS, HALVES, CAP, NY - 1)))
    shapes["zt"] = (dma((ITERS, HALVES, NZ - 1)), dma((ITERS, HALVES, NZ - 1)))
    flat = {}
    for name, shape in shapes.items():
        if isinstance(shape, tuple):
            flat[name + "_s"], flat[name + "_r"] = shape
        else:
            flat[name] = shape
    return flat


def kernel(names, pa_h, pn_h, sh_h, e_h, b_h, c_h, f_h, s_h, i_h, out, *refs):
    r = dict(zip(names, refs))
    tab, loc, half, g_v, p_v, cc = r["tab"], r["loc"], r["half"], r["g_v"], r["p_v"], r["cc"]
    g = lax.axis_index("grp")
    d = lax.axis_index("dev")
    z, y = d // NY, d % NY
    groups = lax.axis_size("grp")
    npno = c_h.shape[1]
    kaux = f_h.shape[0]
    rows = npno // CHUNKS
    part = npno // HALVES
    span_of = [pl.ds(h * part, part) for h in range(HALVES)]

    def at_z(k):
        return {"grp": g, "dev": ((z + k) % NZ) * NY + y}

    def at_y(j):
        return {"grp": g, "dev": z * NY + (y + j) % NY}

    before = {"grp": (g + groups - 1) % groups, "dev": d}
    after = {"grp": (g + 1) % groups, "dev": d}

    sent = []

    def send(src, dst, name, index, where):
        copy = pltpu.make_async_remote_copy(
            src_ref=src, dst_ref=dst,
            send_sem=r[name + "_s"].at[index], recv_sem=r[name + "_r"].at[index],
            device_id=where, device_id_type=MESH,
        )
        copy.start()
        sent.append(copy)
        return copy

    def arrive(copies):
        for copy in copies:
            copy.wait_recv()

    def local(src, dst, number):
        copy = pltpu.make_async_copy(src, dst, loc.at[number])
        copy.start()
        return copy

    own_b = local(b_h, r["b_v"], 0)
    small = [
        local(pa_h, r["pa_s"], 1),
        local(pn_h, r["pn_s"], 2),
        local(sh_h, r["sh_s"], 3),
        local(e_h, r["e_v"], 4),
    ]
    own_c = [local(c_h.at[span_of[h]], r[f"zc0{h}"].at[0], (5, 10, 11, 12)[h]) for h in range(HALVES)]
    own_f = local(f_h, r["f_v"], 6)
    own_s = local(s_h, r["s_v"], 7)
    own_i = local(i_h, r["i_v"], 8)

    barrier = pltpu.get_barrier_semaphore()
    partners = [at_z(k) for k in Z_ORDER] + [at_y(j) for j in Y_ORDER] + [before, after]
    for partner in partners:
        pl.semaphore_signal(barrier, inc=1, device_id=partner, device_id_type=MESH)
    cc[...] = jnp.zeros_like(cc)
    own_b.wait()
    flipped = r["b_v"][...].T
    for c in range(CHUNKS):
        r[f"zb{c}"][0] = flipped[c * rows:(c + 1) * rows]
    for copy in small:
        copy.wait()
    scan_pairs(r["pa_s"], tab, z, y)
    wide = jnp.broadcast_to(r["e_v"][...], (npno, npno))
    r["den"][...] = wide + wide.T + r["sh_s"][0]
    for copy in own_c:
        copy.wait()
    pl.semaphore_wait(barrier, len(partners))

    zb = [{} for c in range(CHUNKS)]

    def direct(c):
        for k in (2, 6, 1, 7):
            zb[c][k] = send(r[f"zb{c}"].at[0], r[f"zb{c}"].at[k], "zb", (c, k - 1), at_z(k))

    def relay(c):
        block = r[f"zb{c}"]
        for held, hop, ahead in ((2, 1, 3), (6, 7, 5)):
            zb[c][held].wait_recv()
            if (held == 2) == (c % 2 == 0):
                zb[c][4] = send(block.at[held], block.at[4], "zb", (c, 3), at_z(held))
            zb[c][ahead] = send(block.at[held], block.at[ahead], "zb", (c, ahead - 1), at_z(hop))

    yb = []

    def cross(c):
        arrive([zb[c][k] for k in (1, 7, 3, 5, 4)])
        for j in Y_ORDER:
            for s in range(CAP):
                r[f"ybo{c}"][j - 1, s] = r[f"zb{c}"][tab[SELK + j * CAP + s]]
            yb.append(
                send(r[f"ybo{c}"].at[j - 1], r[f"yb{c}"].at[j], "yb", (c, j - 1), at_y(j))
            )
        for s in range(CAP):
            r[f"yb{c}"][0, s] = r[f"zb{c}"][tab[SELK + s]]

    for c in range(CHUNKS - 1):
        direct(c)
    relay(0)
    direct(CHUNKS - 1)
    for c in range(1, CHUNKS - 1):
        relay(c)
    cross(0)
    relay(CHUNKS - 1)
    zc = [
        [
            send(c_h.at[span_of[h]], r[f"zc0{h}"].at[k], "zc", (0, h, k - 1), at_z(k))
            for k in Z_ORDER
        ]
        for h in range(HALVES)
    ]
    nx = [send(pn_h, r["n_in"].at[j - 1], "nx", j - 1, at_y(j)) for j in Y_ORDER]
    for c in range(1, CHUNKS):
        cross(c)

    def collect(first, last, lhs):
        height = (last - first) * rows
        for s in range(CAP):
            for c in range(first, last):
                block = r[f"yb{c}"][tab[JSEL + s], s]
                lhs[pl.ds(s * height + (c - first) * rows, rows), :] = block
                r["b_t"][s, pl.ds(c * rows, rows), :] = block

    def first_product(first, last, lhs):
        height = (last - first) * rows

        def step(kk, carry):
            for u in range(BATCH):
                part = jnp.dot(
                    lhs[...], r["f_v"][kk * BATCH + u], preferred_element_type=F32
                ).astype(BF16)
                start = pl.multiple_of(kk * (npno * BATCH), npno * BATCH)
                for s in range(CAP):
                    half[s, pl.ds(start + u * npno + first * rows, height), :] = part[
                        s * height:(s + 1) * height
                    ]
            return carry

        lax.fori_loop(0, kaux // BATCH, step, 0)

    def share_half(it, h, copies, yc, fw):
        column, beside = r[f"zc{it}{h}"], r[f"nc{it}{h}"]
        arrive(copies)
        for s in range(CAP):
            for j in Y_ORDER:
                r[f"yco{it}"][h, s, j - 1] = column[tab[SELK + j * CAP + s]]
            yc[s] += [
                send(
                    r[f"yco{it}"].at[h, s, j - 1], r[f"yc{it}{s}"].at[j, h],
                    "yc", (it, h, s, j - 1), at_y(j),
                )
                for j in Y_ORDER
            ]
            r[f"yc{it}{s}"][0, h] = column[tab[SELK + s]]
        fw.append(send(column, beside.at[pl.ds(NZ, NZ)], "fw", (it, h), before))
        beside[:NZ] = column[...]

    def place(listed):
        return (listed >> 5) * NZ + ((z - ((listed & 31) >> 2)) & (NZ - 1))

    def share_neighbours(it, fw):
        arrive(fw)
        yn = []
        for j in Y_ORDER:
            for n in range(NOV):
                index = place(r["n_s"][NY - 1 - j, 0, n])
                for h in range(HALVES):
                    r[f"yno{it}"][j - 1, n, span_of[h], :] = r[f"nc{it}{h}"][index]
            yn.append(
                send(r[f"yno{it}"].at[j - 1], r[f"yn{it}"].at[j], "yn", (it, j - 1), at_y(j))
            )
        for n in range(NOV):
            index = place(r["pn_s"][0, n])
            for h in range(HALVES):
                r[f"yn{it}"][0, n, span_of[h], :] = r[f"nc{it}{h}"][index]
        return yn

    arrive(nx)
    to_s = local(r["n_in"], r["n_s"], 9)
    own_f.wait()
    arrive(yb[:EARLY * (NY - 1)])
    collect(0, EARLY, r["lhs_a"])
    yc, fw = [[] for s in range(CAP)], []
    first_product(0, EARLY, r["lhs_a"])
    share_half(0, 0, zc[0], yc, fw)
    share_half(0, 1, zc[1], yc, fw)
    arrive(yb[EARLY * (NY - 1):])
    collect(EARLY, CHUNKS, r["lhs_b"])
    first_product(EARLY, CHUNKS, r["lhs_b"])

    def second_product(kk, carry):
        start = pl.multiple_of(kk * (npno * BATCH), npno * BATCH)
        for s in range(CAP):
            inner = lax.dot_general(
                half[s, pl.ds(start, npno * BATCH), :], r["b_t"][s], NT,
                preferred_element_type=F32,
            ).astype(BF16)
            for u in range(BATCH):
                g_v[s, :, pl.ds(start + u * npno, npno)] = inner[u * npno:(u + 1) * npno]
        return carry

    lax.fori_loop(0, kaux // BATCH, second_product, 0)
    to_s.wait()
    own_s.wait()
    own_i.wait()

    for it in range(ITERS):
        yt = [[] for h in range(HALVES)]

        def send_term(s, h):
            home = r[f"yt{it}{h}"]
            for j in Y_ORDER:
                yt[h].append(
                    send(home.at[s], home.at[j * CAP + s], "yt", (it, h, s, j - 1), at_y(j))
                )

        for s in range(CAP):
            arrive(yc[s])
            amps = r[f"yc{it}{s}"][tab[JSEL + s]]
            for h in range(HALVES):
                cc[s, h * part:(h + 1) * part, :npno] = amps[h]
                cc[s, npno + h * part:npno + (h + 1) * part, npno:] = amps[h]
            for b in range(kaux // 2):
                span = pl.ds(b * 2 * npno, 2 * npno)
                p_v[s, :, span] = jnp.dot(
                    g_v[s, :, span], cc[s], preferred_element_type=F32
                ).astype(BF16)
            term = lax.dot_general(p_v[s], g_v[s], NT, preferred_element_type=F32).astype(BF16)
            for h in range(HALVES):
                r[f"yt{it}{h}"][s] = term[h * part:(h + 1) * part]
            for h in range(HALVES if s == 0 else 1):
                send_term(s, h)
        for h in range(1, HALVES):
            for s in range(1, CAP):
                send_term(s, h)
        yn = share_neighbours(it, fw)
        zt = []
        for h in range(HALVES):
            arrive(yt[h])
            copies = []
            for k in Z_ORDER + (0,):
                total = jnp.zeros((part, npno), F32)
                for i in range(2):
                    slot = tab[RET + 2 * k + i]
                    weight = (slot >= 0).astype(F32)
                    total += r[f"yt{it}{h}"][jnp.maximum(slot, 0)].astype(F32) * weight
                if k == 0:
                    r["mine"][span_of[h], :] = total
                else:
                    r[f"bk{it}"][h, k] = total.astype(BF16)
                    copies.append(
                        send(
                            r[f"bk{it}"].at[h, k], r[f"zt{it}"].at[h, k],
                            "zt", (it, h, k - 1), at_z(k),
                        )
                    )
            zt.append(copies)
        arrive(yn)
        coupling = r["i_v"][...]
        for n in range(NOV):
            other = r[f"yn{it}"][(y - (r["pn_s"][0, n] & (NY - 1))) & (NY - 1), n]
            mixed = jnp.dot(r["s_v"][n], other, preferred_element_type=F32).astype(BF16)
            coupling += lax.dot_general(mixed, r["s_v"][n], NT, preferred_element_type=F32)
        r["base"][...] = coupling
        zc = []
        for h in range(HALVES):
            arrive(zt[h])
            total = r["base"][span_of[h], :] + r["mine"][span_of[h], :]
            for k in range(1, NZ):
                total += r[f"zt{it}"][h, k].astype(F32)
            if it + 1 < ITERS:
                column = r[f"zc{it + 1}{h}"]
                column[0] = (-total / r["den"][span_of[h], :]).astype(BF16)
                zc.append([
                    send(column.at[0], column.at[k], "zc", (it + 1, h, k - 1), at_z(k))
                    for k in Z_ORDER
                ])
            else:
                out[span_of[h], :] = total
        if it + 1 < ITERS:
            yc, fw = [[] for s in range(CAP)], []
            for h in range(HALVES):
                share_half(it + 1, h, zc[h], yc, fw)
    for copy in sent:
        copy.wait_send()


def on_device(
    amplitudes,
    bases,
    factors,
    intersections,
    pair_integrals,
    pno_energies,
    pair_shift,
    pair_atoms,
    pair_next,
):
    npno, npao, kaux = amplitudes.shape[1], bases.shape[1], factors.shape[1]
    shapes = scratch(npno, npao, kaux)
    names = tuple(shapes)

    def body(*refs):
        kernel(names, *refs)

    total = pl.pallas_call(
        body,
        out_shape=jax.ShapeDtypeStruct((npno, npno), F32),
        in_specs=[pl.BlockSpec(memory_space=pl.ANY)] * 9,
        out_specs=pl.BlockSpec(memory_space=pltpu.VMEM),
        scratch_shapes=list(shapes.values()),
        compiler_params=pltpu.CompilerParams(
            collective_id=0, has_side_effects=True, vmem_limit_bytes=67043328
        ),
        name="ladder",
    )(
        pair_atoms.T, pair_next, pair_shift, pno_energies, bases[0], amplitudes[0], factors[0],
        intersections[0], pair_integrals[0],
    )
    denominator = pno_energies[0][:, None] + pno_energies[0][None, :] + pair_shift[0]
    return (-total / denominator)[None]


def solution(mesh):
    return jax.shard_map(
        on_device,
        mesh=mesh,
        in_specs=(
            P(("grp", "dev"), None, None),
            P(("grp", "dev"), None, None),
            P(("grp", "dev"), None, None, None),
            P(("grp", "dev"), None, None, None),
            P(("grp", "dev"), None, None),
            P(("grp", "dev"), None),
            P(("grp", "dev")),
            P("grp", None),
            P(("grp", "dev"), None),
        ),
        out_specs=P(("grp", "dev"), None, None),
        check_vma=False,
    )
```
